256 devices in a mesh: row: 2 (over core), col: 64 (over z, y, x_hi), layer: 2 (over x_lo).
Axes of the slice: x: 4 (x_hi: 2, x_lo: 2; x = x_hi * 2 + x_lo), y: 4, z: 8, core: 2. Of those that a mesh axis runs over, the one named last changes fastest.
Arguments:
- u_values: float32 [512, 4, 2, 128, 128], P(('row', 'col'), None, 'layer'), may hold values from -0.1875 to 0.1875
- u_mask: int32 [512, 4, 2], P(('row', 'col'), None, 'layer'), may hold values 0 or 1
- p_values: float32 [256, 2, 8, 128, 128], P(('row', 'col'), 'layer'), may hold values from -6 to 6
- p_mask: int32 [256, 2, 8], P(('row', 'col'), 'layer'), may hold values 0 or 1
- t_mask: int32 [512, 4, 2], P(('row', 'col'), None, 'layer'), may hold values 0 or 1
- out_mask: int32 [256, 2, 8], P(('row', 'col'), 'layer'), may hold values 0 or 1
Outputs:
- new_density: float32 [256, 2, 8, 128, 128], P(('row', 'col'), 'layer')
The draws below stay inside these ranges and needn't reach their ends.
All inputs are finite; a program needn't handle non-finite values. No bound on the sum of `u_mask` or of `p_mask` or of `t_mask` or of `out_mask` on one device may be relied on, other than what follows from the above.
Results may differ from the reference program's by a relative error of at most 0.0001.
Values sent between devices are 32-bit elements; how exact they have to be, the bound alone decides.
A program may use at most 64 MiB of HBM per device.

```python
import jax
import jax.numpy as jnp
from jax import lax

BLK = 128
NO = 8
REACH = 4
NB = 512
N_LAYER = 2


def set_ends(values, rng, least, high):
    extent = values.shape
    spot = [jax.random.randint(jax.random.fold_in(rng, axis), (), 0, extent[axis]) for axis in range(len(extent))]
    values = values.at[tuple(spot)].set(least)
    longest = extent.index(max(extent))
    spot[longest] = (spot[longest] + 1) % extent[longest]
    return values.at[tuple(spot)].set(high)


def levels(stream_key, dims, split, low, high):
    factor_of = 1.0
    for axis_at, shards_of in split:
        draws = jax.random.uniform(jax.random.fold_in(jax.random.fold_in(stream_key, 6), axis_at), (shards_of,), jnp.float32, low / len(split), high / len(split))
        factor_of = factor_of * jnp.repeat(jnp.exp(draws), dims[axis_at] // shards_of).reshape((-1,) + (1,) * (len(dims) - 1 - axis_at))
    return factor_of


def bell_draw(key, shape, deviation, reach, split=(), held_as=jnp.bfloat16):
    entries = jax.random.normal(key, shape, jnp.float32) * deviation
    if len(split) > 0:
        entries = levels(key, shape, split, -0.22, 0.18) * entries
    return jnp.clip(entries, min=-reach, max=reach).astype(held_as)


def setup_inputs(seed: int = 0) -> dict:
    seeds = jax.random.split(jax.random.key(seed), 7)
    return {
        "u_values": bell_draw(seeds[0], (NB, NO // N_LAYER, N_LAYER, BLK, BLK), (NO * BLK) ** -0.5, 0.1875, ((0, 128), (2, 2)), jnp.float32),
        "u_mask": set_ends((jax.random.randint(seeds[1], (NB, NO // N_LAYER, N_LAYER), 0, 5) < 3).astype(jnp.int32), jax.random.fold_in(seeds[1], 1), 0, 1),
        "p_values": bell_draw(seeds[2], (NB // N_LAYER, N_LAYER, NO, BLK, BLK), 1.0, 6.0, ((0, 128), (1, 2)), jnp.float32),
        "p_mask": set_ends((jax.random.randint(seeds[3], (NB // N_LAYER, N_LAYER, NO), 0, 5) < 3).astype(jnp.int32), jax.random.fold_in(seeds[3], 1), 0, 1),
        "t_mask": set_ends((jax.random.randint(seeds[4], (NB, NO // N_LAYER, N_LAYER), 0, 5) < 3).astype(jnp.int32), jax.random.fold_in(seeds[4], 1), 0, 1),
        "out_mask": set_ends((jax.random.randint(seeds[5], (NB // N_LAYER, N_LAYER, NO), 0, 5) < 3).astype(jnp.int32), jax.random.fold_in(seeds[5], 1), 0, 1),
    }


def class_to_offset(source):
    parted = source.reshape((NB // N_LAYER, N_LAYER) + source.shape[1:])
    rolled = [jnp.roll(parted[:, r], -r, axis=2) for r in range(N_LAYER)]
    stacked = jnp.stack(rolled, axis=1)
    return stacked.reshape((NB, NO) + source.shape[3:])


def band_valid():
    row_index = jnp.arange(NB, dtype=jnp.int32)[:, None]
    offsets = jnp.arange(NO, dtype=jnp.int32)[None, :]
    column = row_index - REACH + offsets
    return ((column >= 0) & (column < NB)).astype(jnp.float32)


def reference(u_values, u_mask, p_values, p_mask, t_mask, out_mask):
    valid = band_valid()
    u_keep = class_to_offset(u_mask).astype(jnp.float32) * valid
    u_band = class_to_offset(u_values) * u_keep[:, :, None, None]
    p_keep = p_mask.reshape(NB, NO).astype(jnp.float32) * valid
    p_band = p_values.reshape(NB, NO, BLK, BLK) * p_keep[:, :, None, None]
    p_padded = jnp.pad(p_band, ((REACH, REACH), (0, 0), (0, 0), (0, 0)))
    product = jnp.zeros((NB, NO, BLK, BLK), jnp.float32)
    for ou in range(NO):
        low = max(0, REACH - ou)
        high = min(NO, NO + REACH - ou)
        p_rows = p_padded[ou:ou + NB, low:high]
        term = jnp.einsum("iab,iobc->ioac", u_band[:, ou], p_rows, precision=lax.Precision.HIGHEST)
        product = product.at[:, ou + low - REACH:ou + high - REACH].add(term)
    t_keep = class_to_offset(t_mask).astype(jnp.float32) * valid
    product = product * t_keep[:, :, None, None]
    u_padded = jnp.pad(u_band, ((REACH, REACH), (0, 0), (0, 0), (0, 0)))
    columns = []
    for op in range(NO):
        low = max(0, op - REACH)
        high = min(NO, NO + op - REACH)
        u_rows = u_padded[op:op + NB, low - op + REACH:high - op + REACH]
        columns.append(jnp.einsum("ioab,iocb->iac", product[:, low:high], u_rows, precision=lax.Precision.HIGHEST))
    result = jnp.stack(columns, axis=1)
    o_keep = out_mask.reshape(NB, NO).astype(jnp.float32) * valid
    result = result * o_keep[:, :, None, None]
    return result.reshape(NB // N_LAYER, N_LAYER, NO, BLK, BLK)
```

```python
import functools

import jax
import jax.numpy as jnp
from jax import lax
from jax.experimental import pallas as pl
from jax.experimental.pallas import tpu as pltpu
from jax.sharding import PartitionSpec as P

B = 128
NO = 8
F32 = jnp.float32
BF16 = jnp.bfloat16
MESH = pl.DeviceIdType.MESH

S0_P, S0_U, S0_M = 0, 4, 8
S1_P, S1_U, S1_M = 9, 13, 17
H_P, H_UX, H_UY = 18, 24, 30
OUT = 36
COPIES = 52

REACH = {
    0: (True, 4, 4, 2, 2, 2, 2),
    1: (True, 3, 5, 2, 2, 1, 3),
    2: (True, 2, 6, 1, 3, 1, 3),
    8: (False, 0, 6, 0, 3, 0, 3),
    9: (False, 0, 5, 0, 3, 0, 2),
}
SLOT = {0: 0, 1: 1, 2: 2, 8: 3, 9: 4, "s": 5}


def split(x):
    high = x.astype(BF16)
    return high, (x - high.astype(F32)).astype(BF16)


def dot(a, b):
    return jnp.dot(a, b, preferred_element_type=F32)


def dot_t(a, b):
    return lax.dot_general(a, b, (((1,), (1,)), ((), ())), preferred_element_type=F32)


def kernel(cols, um, pm, tm, om, u_in, p_in, out, ub, pb, mb, su, sp, sm, t2, th, tl, ob,
           send, recv, local):
    core = lax.axis_index("row")
    col = lax.axis_index("col")
    layer = lax.axis_index("layer")
    half = col % 2
    quad = col // 2
    quads = cols // 2
    lam = (layer + core + half) % 2
    swaps = (core + half) % 2
    slabs = 4 * quads
    total = 4 * slabs
    first_row = 4 * (core * cols + col)

    def place(index):
        index = (index + slabs) % slabs
        h = index % 2
        q = index // 2
        p = q // quads
        return (h, (q % quads) * 2 + p, (1 - lam + h + p) % 2)

    chain = (half * quads + quad) * 2 + core
    up = place(chain + 1)
    down = place(chain - 1)
    partner = (core, col, 1 - layer)
    pair = (1 - core, quad * 2 + 1 - half, 1 - layer)

    def remote(src, dst, number, device):
        return pltpu.make_async_remote_copy(
            src_ref=src, dst_ref=dst, send_sem=send.at[number], recv_sem=recv.at[number],
            device_id=device, device_id_type=MESH)

    started = []

    def push(src, dst, number, device):
        copy = remote(src, dst, number, device)
        copy.start()
        started.append(copy)

    def got(view, number):
        remote(view, view, number, partner).wait_recv()

    def move(src, dst, number):
        @pl.when(swaps == 1)
        def _():
            remote(src, dst, number, pair).start()

        @pl.when(swaps == 0)
        def _():
            pltpu.make_async_copy(src, dst, local.at[number]).start()

    def moved(src, dst, number):
        @pl.when(swaps == 1)
        def _():
            remote(src, dst, number, pair).wait()

        @pl.when(swaps == 0)
        def _():
            pltpu.make_async_copy(src, dst, local.at[number]).wait()

    def keep(mask, index, column):
        ok = (column >= 0) & (column < total)
        return jnp.where(ok, mask[index], 0).astype(F32)

    def p_chunk(cls, c):
        return pb.at[4 + cls + 2 * (c // 2), pl.ds(4 * (c % 2), 4)]

    def u_chunk(cls, c):
        row = [1 - cls, 3 - cls, cls, cls + 2][c]
        return ub.at[4 + row, [1, 1, 0, 0][c]]

    barrier = pltpu.get_barrier_semaphore()
    for device in (partner, up, down):
        pl.semaphore_signal(barrier, inc=1, device_id=device, device_id_type=MESH)

    @pl.when(swaps == 1)
    def _():
        pl.semaphore_signal(barrier, inc=1, device_id=pair, device_id_type=MESH)

    def stage_p(c):
        a, o0 = c // 2, 4 * (c % 2)

        @pl.loop(0, 4)
        def _(s):
            column = first_row + layer + 2 * a - 4 + o0 + s
            sp[c, s] = p_in[a, o0 + s] * keep(pm, a * 8 + o0 + s, column)

    def stage_u(c):
        row = [1 - layer, 3 - layer, layer, layer + 2][c]

        @pl.loop(0, 4)
        def _(s):
            column = first_row + row - 4 + [1, 1, 0, 0][c] + 2 * s
            su[c, s] = u_in[row, s] * keep(um, row * 4 + s, column)

    @pl.loop(0, 16)
    def _(s):
        row, m = s // 4, s % 4
        column = first_row + row - 4 + (layer + row) % 2 + 2 * m
        sm[0, pl.ds(s, 1), :] = jnp.full((1, B), keep(tm, s, column), F32)
        a, o = s // 8, s % 8
        column = first_row + layer + 2 * a - 4 + o
        sm[1, pl.ds(s, 1), :] = jnp.full((1, B), keep(om, s, column), F32)

    stage_p(0)
    pl.semaphore_wait(barrier, 3 + swaps)
    move(sp.at[0], p_chunk(layer, 0), S0_P)
    for c in range(1, 4):
        stage_p(c)
        move(sp.at[c], p_chunk(layer, c), S0_P + c)
    move(sm, mb.at[pl.ds(0, 2)], S0_M)
    for c in range(4):
        stage_u(c)
        move(su.at[c], u_chunk(layer, c), S0_U + c)

    def reach_p(key):
        if key == "s":
            push(pb.at[4 + 3 * lam, pl.ds(lam, 7)], pb.at[8 - 5 * lam, pl.ds(lam, 7)],
                 H_P + SLOT[key], special)
            return
        goes_up, o0, n = REACH[key][:3]
        row = key + 1 - lam if goes_up else key - 7 - lam
        push(pb.at[4 + row, pl.ds(o0, n)], pb.at[row if goes_up else 8 + row, pl.ds(o0, n)],
             H_P + SLOT[key], up if goes_up else down)

    def got_p(key):
        if key == "s":
            got(pb.at[3 + 5 * lam, pl.ds(1 - lam, 7)], H_P + SLOT[key])
            return
        _, o0, n = REACH[key][:3]
        got(pb.at[key + lam, pl.ds(o0, n)], H_P + SLOT[key])

    def u_slots(key, parity):
        return REACH[key][3 + 2 * parity], REACH[key][4 + 2 * parity]

    def reach_u(key, cls):
        base = H_UX if cls == "x" else H_UY
        if key == "s":
            parity = 0 if cls == "x" else 1
            push(ub.at[4 + 3 * lam, parity], ub.at[8 - 5 * lam, parity],
                 base + SLOT[key], special)
            return
        goes_up = REACH[key][0]
        parity = (key + 1) % 2 if cls == "x" else key % 2
        m0, n = u_slots(key, parity)
        row = key + 1 - lam if goes_up else key - 7 - lam
        push(ub.at[4 + row, parity, pl.ds(m0, n)],
             ub.at[row if goes_up else 8 + row, parity, pl.ds(m0, n)],
             base + SLOT[key], up if goes_up else down)

    def got_u(key):
        for cls in ("x", "y"):
            base = H_UX if cls == "x" else H_UY
            if key == "s":
                got(ub.at[3 + 5 * lam, 0 if cls == "x" else 1], base + SLOT[key])
                continue
            parity = (key + 1) % 2 if cls == "x" else key % 2
            m0, n = u_slots(key, parity)
            got(ub.at[key + lam, parity, pl.ds(m0, n)], base + SLOT[key])

    special = tuple(jnp.where(lam == 1, a, b) for a, b in zip(up, down))

    for c in range(4):
        moved(sp.at[c], p_chunk(lam, c), S0_P + c)
        push(p_chunk(lam, c), p_chunk(lam, c), S1_P + c, partner)
    moved(sm, mb.at[pl.ds(0, 2)], S0_M)
    push(mb.at[0], mb.at[2], S1_M, partner)
    for key in ("s", 1, 9):
        reach_p(key)

    after = {0: (0, 8), 1: (2,), 3: ("s", 1, 9)}
    for c in range(4):
        moved(su.at[c], u_chunk(lam, c), S0_U + c)
        push(u_chunk(lam, c), u_chunk(lam, c), S1_U + c, partner)
        for key in after.get(c, ()):
            reach_u(key, "x")

    t2[...] = jnp.zeros_like(t2)

    for c in range(4):
        got(p_chunk(1 - lam, c), S1_P + c)
        if c == 1:
            reach_p(0)
            reach_p(8)
        if c == 3:
            reach_p(2)

    def t_step(k):
        lo, hi = max(0, k - 4), min(9, k + 3)
        width = hi - lo + 1
        rows = []
        if k < 8:
            rows.append(ub[4 + lam, k % 2, k // 2])
        if k >= 2:
            rows.append(ub[6 + lam, k % 2, (k - 2) // 2])
        a = rows[0] if len(rows) == 1 else jnp.concatenate(rows, axis=0)
        r0, r1 = (0 if k < 8 else B), (2 * B if k >= 2 else B)
        ah, al = split(a)
        both = jnp.concatenate([ah, al], axis=1)
        for w0 in range(0, width, 4):
            w1 = min(width, w0 + 4)
            b = jnp.concatenate(
                [pb[k + lam, lo + w - k + 4] for w in range(w0, w1)], axis=1)
            bh, bl = split(b)
            value = dot(both, jnp.concatenate([bh, bh], axis=0)) + dot(ah, bl)
            t2[r0:r1, (lo + w0) * B:(lo + w1) * B] += value

    def o_step(k):
        lo, hi = max(0, k - 4), min(9, k + 3)
        r0, r1 = (0 if k < 8 else B), (2 * B if k >= 2 else B)
        b = jnp.concatenate(
            [ub[lam + k, (j - k + 4) % 2, (j - k + 4) // 2] for j in range(lo, hi + 1)], axis=1)
        bh, bl = split(b)
        window = slice(lo * B, (hi + 1) * B)
        ah = th[r0:r1, window]
        value = dot_t(ah, bh) + dot_t(ah, bl) + dot_t(tl[r0:r1, window], bh)
        for a in range(2):
            o = k - 2 * a
            if 0 <= o < NO:
                block = value[a * B - r0:(a + 1) * B - r0]
                ob[a, o] = block * mb[1, pl.ds(a * 8 + o, 1), :]
                move_out(a, o)

    def move_out(a, o):
        move(ob.at[a, o], out.at[a, 0, o], OUT + a * 8 + o)

    t_step(4)
    t_step(6)
    for key in (0, 2, 8):
        got_p(key)
        t_step(key)

    got(u_chunk(1 - lam, 0), S1_U)
    got(u_chunk(1 - lam, 1), S1_U + 1)
    for key in ("s", 1, 9):
        reach_u(key, "y")
    t_step(5)
    got_p("s")
    t_step(3)
    t_step(7)
    got_p(1)
    t_step(1)
    got_p(9)
    t_step(9)

    got(mb.at[2], S1_M)
    for a in range(2):
        for j in range(10):
            o = j - 2 * a
            spot = (slice(a * B, (a + 1) * B), slice(j * B, (j + 1) * B))
            if 0 <= o < NO:
                row = (lam + 2 * a) * 4 + o // 2
                value = t2[spot] * mb[0 if o % 2 == 0 else 2, pl.ds(row, 1), :]
                high, low = split(value)
            else:
                high = low = jnp.zeros((B, B), BF16)
            th[spot] = high
            tl[spot] = low

    got(u_chunk(1 - lam, 2), S1_U + 2)
    reach_u(0, "y")
    reach_u(8, "y")
    o_step(4)
    o_step(6)
    got(u_chunk(1 - lam, 3), S1_U + 3)
    reach_u(2, "y")
    got_u("s")
    for key in (5, 3, 7):
        o_step(key)
    for key in (1, 9, 0, 8, 2):
        got_u(key)
        o_step(key)

    for a in range(2):
        for o in range(NO):
            moved(ob.at[a, o], out.at[a, 0, o], OUT + a * 8 + o)
    for copy in started:
        copy.wait_send()


def on_device(cols, u_values, u_mask, p_values, p_mask, t_mask, out_mask):
    smem = pl.BlockSpec(memory_space=pltpu.SMEM)
    vmem = pl.BlockSpec(memory_space=pltpu.VMEM)
    return pl.pallas_call(
        functools.partial(kernel, cols),
        out_shape=jax.ShapeDtypeStruct((2, 1, NO, B, B), F32),
        in_specs=[smem] * 4 + [vmem] * 2,
        out_specs=pl.BlockSpec(memory_space=pl.ANY),
        scratch_shapes=[
            pltpu.VMEM((12, 2, 4, B, B), F32),
            pltpu.VMEM((12, NO, B, B), F32),
            pltpu.VMEM((3, 16, B), F32),
            pltpu.VMEM((4, 4, B, B), F32),
            pltpu.VMEM((4, 4, B, B), F32),
            pltpu.VMEM((2, 16, B), F32),
            pltpu.VMEM((2 * B, 10 * B), F32),
            pltpu.VMEM((2 * B, 10 * B), BF16),
            pltpu.VMEM((2 * B, 10 * B), BF16),
            pltpu.VMEM((2, NO, B, B), F32),
            pltpu.SemaphoreType.DMA((COPIES,)),
            pltpu.SemaphoreType.DMA((COPIES,)),
            pltpu.SemaphoreType.DMA((COPIES,)),
        ],
        compiler_params=pltpu.CompilerParams(
            collective_id=0, has_side_effects=True, vmem_limit_bytes=48 << 20),
        cost_estimate=pl.CostEstimate(
            flops=2 * 192 * B**3, bytes_accessed=3 << 20, transcendentals=0),
    )(
        u_mask.reshape(16), p_mask.reshape(16), t_mask.reshape(16), out_mask.reshape(16),
        u_values.reshape(4, 4, B, B), p_values.reshape(2, NO, B, B),
    )


def solution(mesh):
    placed = (
        P(("row", "col"), None, "layer", None, None),
        P(("row", "col"), None, "layer"),
        P(("row", "col"), "layer", None, None, None),
        P(("row", "col"), "layer", None),
        P(("row", "col"), None, "layer"),
        P(("row", "col"), "layer", None),
    )
    return jax.shard_map(
        functools.partial(on_device, mesh.shape["col"]),
        mesh=mesh,
        in_specs=placed,
        out_specs=P(("row", "col"), "layer", None, None, None),
        check_vma=False,
    )
```

```python
import functools

import jax
import jax.numpy as jnp
from jax import lax
from jax.experimental import pallas as pl
from jax.experimental.pallas import tpu as pltpu
from jax.sharding import PartitionSpec as P

B = 128
NO = 8
F32 = jnp.float32
BF16 = jnp.bfloat16
MESH = pl.DeviceIdType.MESH

S0_P, S0_U, S0_M = 0, 4, 8
S1_P, S1_U, S1_M = 9, 13, 17
H_P, H_UX, H_UY = 18, 24, 30
OUT = 36
COPIES = 52

REACH = {
    0: (True, 4, 4, 2, 2, 2, 2),
    1: (True, 3, 5, 2, 2, 1, 3),
    2: (True, 2, 6, 1, 3, 1, 3),
    8: (False, 0, 6, 0, 3, 0, 3),
    9: (False, 0, 5, 0, 3, 0, 2),
}
SLOT = {0: 0, 1: 1, 2: 2, 8: 3, 9: 4, "s": 5}


def split(x):
    high = x.astype(BF16)
    return high, (x - high.astype(F32)).astype(BF16)


def dot(a, b):
    return jnp.dot(a, b, preferred_element_type=F32)


def dot_t(a, b):
    return lax.dot_general(a, b, (((1,), (1,)), ((), ())), preferred_element_type=F32)


def kernel(cols, um, pm, tm, om, u_in, p_in, out, ub, pb, mb, su, sp, sm, t2, th, tl, ob,
           send, recv, local, load):
    core = lax.axis_index("row")
    col = lax.axis_index("col")
    layer = lax.axis_index("layer")
    half = col % 2
    quad = col // 2
    quads = cols // 2
    lam = (layer + core + half) % 2
    swaps = (core + half) % 2
    slabs = 4 * quads
    total = 4 * slabs
    first_row = 4 * (core * cols + col)

    def place(index):
        index = (index + slabs) % slabs
        h = index % 2
        q = index // 2
        p = q // quads
        return (h, (q % quads) * 2 + p, (1 - lam + h + p) % 2)

    chain = (half * quads + quad) * 2 + core
    up = place(chain + 1)
    down = place(chain - 1)
    partner = (core, col, 1 - layer)
    pair = (1 - core, quad * 2 + 1 - half, 1 - layer)

    def remote(src, dst, number, device):
        return pltpu.make_async_remote_copy(
            src_ref=src, dst_ref=dst, send_sem=send.at[number], recv_sem=recv.at[number],
            device_id=device, device_id_type=MESH)

    started = []

    def push(src, dst, number, device, ok=None):
        copy = remote(src, dst, number, device)
        started.append((copy, ok))
        if ok is None:
            copy.start()
        else:
            pl.when(ok)(copy.start)

    def got(view, number, ok=None):
        copy = remote(view, view, number, partner)
        if ok is None:
            copy.wait_recv()
        else:
            pl.when(ok)(copy.wait_recv)

    def move(src, dst, number):
        @pl.when(swaps == 1)
        def _():
            remote(src, dst, number, pair).start()

        @pl.when(swaps == 0)
        def _():
            pltpu.make_async_copy(src, dst, local.at[number]).start()

    def moved(src, dst, number):
        @pl.when(swaps == 1)
        def _():
            remote(src, dst, number, pair).wait()

        @pl.when(swaps == 0)
        def _():
            pltpu.make_async_copy(src, dst, local.at[number]).wait()

    def keep(mask, index, column):
        ok = (column >= 0) & (column < total)
        return jnp.where(ok, mask[index], 0).astype(F32)

    last = quads - 1
    lower = chain != 0
    upper = chain != slabs - 1
    x_up = (core != 1) | (quad != last)
    x_down = (core != 0) | (quad != 0)
    edge = (swaps == 1) & ((quad == 0) | (quad == last))
    stand_up = edge & (half == 1) & (quad == last)
    stand_down = edge & (half == 0) & (quad == 0)
    mate = (core, (last - quad) * 2 + half, layer)

    def p_chunk(cls, c):
        return pb.at[4 + cls + 2 * (c // 2), pl.ds(4 * (c % 2), 4)]

    def u_chunk(cls, c):
        row = [1 - cls, 3 - cls, cls, cls + 2][c]
        return ub.at[4 + row, [1, 1, 0, 0][c]]

    barrier = pltpu.get_barrier_semaphore()
    for device in (partner, up, down):
        pl.semaphore_signal(barrier, inc=1, device_id=device, device_id_type=MESH)

    @pl.when(swaps == 1)
    def _():
        pl.semaphore_signal(barrier, inc=1, device_id=pair, device_id_type=MESH)

    @pl.when(edge)
    def _():
        pl.semaphore_signal(barrier, inc=1, device_id=mate, device_id_type=MESH)

    def p_stage(c):
        return sp.at[c // 2, pl.ds(4 * (c % 2), 4)]

    def u_row(c):
        return [1 - layer, 3 - layer, layer, layer + 2][c]

    def loads(c):
        yield pltpu.make_async_copy(
            p_in.at[c // 2, 0, pl.ds(4 * (c % 2), 4)], p_stage(c), load.at[c])
        yield pltpu.make_async_copy(
            u_in.at[u_row(c), pl.ds(0, 4), 0], su.at[c], load.at[4 + c])

    p_loads, u_loads = zip(*[tuple(loads(c)) for c in range(4)])
    for copy in p_loads + u_loads:
        copy.start()

    def stage_p(c):
        a, o0 = c // 2, 4 * (c % 2)
        p_loads[c].wait()

        def value(s):
            column = first_row + layer + 2 * a - 4 + o0 + s
            return sp[a, o0 + s] * keep(pm, (a, 0, o0 + s), column)

        @pl.when(swaps == 0)
        def _():
            @pl.loop(0, 4)
            def _(s):
                pb[4 + layer + 2 * a, o0 + s] = value(s)

        @pl.when(swaps == 1)
        def _():
            @pl.loop(0, 4)
            def _(s):
                sp[a, o0 + s] = value(s)

            remote(p_stage(c), p_chunk(layer, c), S0_P + c, pair).start()

    def stage_u(c):
        row = u_row(c)
        u_loads[c].wait()

        def value(s):
            column = first_row + row - 4 + [1, 1, 0, 0][c] + 2 * s
            return su[c, s] * keep(um, (row, 0, s), column)

        @pl.when(swaps == 0)
        def _():
            @pl.loop(0, 4)
            def _(s):
                ub[4 + row, [1, 1, 0, 0][c], s] = value(s)

        @pl.when(swaps == 1)
        def _():
            @pl.loop(0, 4)
            def _(s):
                su[c, s] = value(s)

            remote(su.at[c], u_chunk(layer, c), S0_U + c, pair).start()

    def swapped(view, number):
        @pl.when(swaps == 1)
        def _():
            remote(view, view, number, pair).wait_recv()

    @pl.loop(0, 16)
    def _(s):
        row, m = s // 4, s % 4
        column = first_row + row - 4 + (layer + row) % 2 + 2 * m
        sm[0, pl.ds(s, 1), :] = jnp.full((1, B), keep(tm, (row, 0, m), column), F32)
        a, o = s // 8, s % 8
        column = first_row + layer + 2 * a - 4 + o
        sm[1, pl.ds(s, 1), :] = jnp.full((1, B), keep(om, (a, 0, o), column), F32)

    def clear(row):
        @pl.loop(row, row + 4)
        def _(r):
            @pl.loop(0, NO)
            def _(o):
                pb[r, o] = jnp.zeros((B, B), F32)
                ub[r, o // 4, o % 4] = jnp.zeros((B, B), F32)

    @pl.when(chain == 0)
    def _():
        clear(0)

    @pl.when(chain == slabs - 1)
    def _():
        clear(8)

    pl.semaphore_wait(barrier, 3 + swaps + edge.astype(jnp.int32))
    for c in range(4):
        stage_p(c)
    move(sm, mb.at[pl.ds(0, 2)], S0_M)
    for c in range(4):
        stage_u(c)

    def may_send(key, cls):
        above, below = (x_up, x_down) if cls == "x" else (upper, lower)
        if key == "s":
            return ((lam == 1) & above) | ((lam == 0) & below)
        return above if REACH[key][0] else below

    def comes(key):
        if key == "s":
            return ((lam == 0) & lower) | ((lam == 1) & upper)
        return lower if REACH[key][0] else upper

    def stand_in(key, kind):
        goes_up = REACH[key][0] if key != "s" else None
        if key == "s":
            ok = (stand_up & (layer == 1)) | (stand_down & (layer == 0))
        else:
            ok = stand_up if goes_up else stand_down
        number = (H_P if kind == "p" else H_UX) + SLOT[key]

        @pl.when(ok)
        def _():
            stand_copy(key, kind, number).start()

        stood.append((key, kind, number, ok))

    stood = []

    def stand_copy(key, kind, number):
        if key == "s":
            source, place_row = None, 8 - 5 * layer
        else:
            goes_up = REACH[key][0]
            source = key + 1 - layer if goes_up else key - 7 - layer
            place_row = source if goes_up else 8 + source
        if kind == "p":
            a = layer if key == "s" else 1 - layer
            blocks = pl.ds(layer, 7) if key == "s" else pl.ds(*REACH[key][1:3])
            return remote(sp.at[a, blocks], pb.at[place_row, blocks], number, mate)
        c = {"s": 2 + layer, 0: 0, 8: 0, 2: 1, 1: 3 - layer, 9: 3 - layer}[key]
        parity = 0 if key == "s" else (key + 1) % 2
        slots = pl.ds(0, 4) if key == "s" else pl.ds(*u_slots(key, parity))
        return remote(su.at[c, slots], ub.at[place_row, parity, slots], number, mate)

    def reach_p(key):
        if key == "s":
            push(pb.at[4 + 3 * lam, pl.ds(lam, 7)], pb.at[8 - 5 * lam, pl.ds(lam, 7)],
                 H_P + SLOT[key], special, may_send(key, "x"))
            return
        goes_up, o0, n = REACH[key][:3]
        row = key + 1 - lam if goes_up else key - 7 - lam
        push(pb.at[4 + row, pl.ds(o0, n)], pb.at[row if goes_up else 8 + row, pl.ds(o0, n)],
             H_P + SLOT[key], up if goes_up else down,
             may_send(key, "x" if key in (1, 9) else "y"))

    def got_p(key):
        if key == "s":
            got(pb.at[3 + 5 * lam, pl.ds(1 - lam, 7)], H_P + SLOT[key], comes(key))
            return
        _, o0, n = REACH[key][:3]
        got(pb.at[key + lam, pl.ds(o0, n)], H_P + SLOT[key], comes(key))

    def u_slots(key, parity):
        return REACH[key][3 + 2 * parity], REACH[key][4 + 2 * parity]

    def reach_u(key, cls):
        base = H_UX if cls == "x" else H_UY
        if key == "s":
            parity = 0 if cls == "x" else 1
            push(ub.at[4 + 3 * lam, parity], ub.at[8 - 5 * lam, parity],
                 base + SLOT[key], special, may_send(key, cls))
            return
        goes_up = REACH[key][0]
        parity = (key + 1) % 2 if cls == "x" else key % 2
        m0, n = u_slots(key, parity)
        row = key + 1 - lam if goes_up else key - 7 - lam
        push(ub.at[4 + row, parity, pl.ds(m0, n)],
             ub.at[row if goes_up else 8 + row, parity, pl.ds(m0, n)],
             base + SLOT[key], up if goes_up else down, may_send(key, cls))

    def got_u(key):
        for cls in ("x", "y"):
            base = H_UX if cls == "x" else H_UY
            if key == "s":
                got(ub.at[3 + 5 * lam, 0 if cls == "x" else 1], base + SLOT[key], comes(key))
                continue
            parity = (key + 1) % 2 if cls == "x" else key % 2
            m0, n = u_slots(key, parity)
            got(ub.at[key + lam, parity, pl.ds(m0, n)], base + SLOT[key], comes(key))

    special = tuple(jnp.where(lam == 1, a, b) for a, b in zip(up, down))

    for c in range(4):
        swapped(p_chunk(lam, c), S0_P + c)
        push(p_chunk(lam, c), p_chunk(lam, c), S1_P + c, partner)
    moved(sm, mb.at[pl.ds(0, 2)], S0_M)
    push(mb.at[0], mb.at[2], S1_M, partner)
    for key in ("s", 1, 9):
        reach_p(key)
        stand_in(key, "p")

    after = {0: (0, 8), 1: (2,), 3: ("s", 1, 9)}
    for c in range(4):
        swapped(u_chunk(lam, c), S0_U + c)
        push(u_chunk(lam, c), u_chunk(lam, c), S1_U + c, partner)
        for key in after.get(c, ()):
            reach_u(key, "x")
            stand_in(key, "u")

    t2[...] = jnp.zeros_like(t2)

    for c in range(4):
        got(p_chunk(1 - lam, c), S1_P + c)
        if c == 1:
            reach_p(0)
            reach_p(8)
        if c == 3:
            reach_p(2)

    def t_step(k):
        lo, hi = max(0, k - 4), min(9, k + 3)
        width = hi - lo + 1
        rows = []
        if k < 8:
            rows.append(ub[4 + lam, k % 2, k // 2])
        if k >= 2:
            rows.append(ub[6 + lam, k % 2, (k - 2) // 2])
        a = rows[0] if len(rows) == 1 else jnp.concatenate(rows, axis=0)
        r0, r1 = (0 if k < 8 else B), (2 * B if k >= 2 else B)
        ah, al = split(a)
        both = jnp.concatenate([ah, al], axis=1)
        for w0 in range(0, width, 4):
            w1 = min(width, w0 + 4)
            b = jnp.concatenate(
                [pb[k + lam, lo + w - k + 4] for w in range(w0, w1)], axis=1)
            bh, bl = split(b)
            value = dot(both, jnp.concatenate([bh, bh], axis=0)) + dot(ah, bl)
            t2[r0:r1, (lo + w0) * B:(lo + w1) * B] += value

    def o_step(k):
        lo, hi = max(0, k - 4), min(9, k + 3)
        r0, r1 = (0 if k < 8 else B), (2 * B if k >= 2 else B)
        b = jnp.concatenate(
            [ub[lam + k, (j - k + 4) % 2, (j - k + 4) // 2] for j in range(lo, hi + 1)], axis=1)
        bh, bl = split(b)
        window = slice(lo * B, (hi + 1) * B)
        ah = th[r0:r1, window]
        value = dot_t(ah, bh) + dot_t(ah, bl) + dot_t(tl[r0:r1, window], bh)
        for a in range(2):
            o = k - 2 * a
            if 0 <= o < NO:
                block = value[a * B - r0:(a + 1) * B - r0]
                ob[a, o] = block * mb[1, pl.ds(a * 8 + o, 1), :]
                move_out(a, o)

    def move_out(a, o):
        move(ob.at[a, o], out.at[a, 0, o], OUT + a * 8 + o)

    t_step(4)
    t_step(6)
    for key in (0, 2, 8):
        got_p(key)
        t_step(key)

    got(u_chunk(1 - lam, 0), S1_U)
    got(u_chunk(1 - lam, 1), S1_U + 1)
    for key in ("s", 1, 9):
        reach_u(key, "y")
    t_step(5)
    got_p("s")
    t_step(3)
    t_step(7)
    got_p(1)
    t_step(1)
    got_p(9)
    t_step(9)

    got(mb.at[2], S1_M)
    for a in range(2):
        for j in range(10):
            o = j - 2 * a
            spot = (slice(a * B, (a + 1) * B), slice(j * B, (j + 1) * B))
            if 0 <= o < NO:
                row = (lam + 2 * a) * 4 + o // 2
                value = t2[spot] * mb[0 if o % 2 == 0 else 2, pl.ds(row, 1), :]
                high, low = split(value)
            else:
                high = low = jnp.zeros((B, B), BF16)
            th[spot] = high
            tl[spot] = low

    got(u_chunk(1 - lam, 2), S1_U + 2)
    reach_u(0, "y")
    reach_u(8, "y")
    o_step(4)
    o_step(6)
    got(u_chunk(1 - lam, 3), S1_U + 3)
    reach_u(2, "y")
    got_u("s")
    for key in (5, 3, 7):
        o_step(key)
    for key in (1, 9, 0, 8, 2):
        got_u(key)
        o_step(key)

    for a in range(2):
        for o in range(NO):
            moved(ob.at[a, o], out.at[a, 0, o], OUT + a * 8 + o)
    for c in range(4):
        @pl.when(swaps == 1)
        def _():
            remote(p_stage(c), p_stage(c), S0_P + c, pair).wait_send()
            remote(su.at[c], su.at[c], S0_U + c, pair).wait_send()
    for copy, ok in started:
        if ok is None:
            copy.wait_send()
        else:
            pl.when(ok)(copy.wait_send)
    for key, kind, number, ok in stood:
        @pl.when(ok)
        def _():
            stand_copy(key, kind, number).wait_send()


def on_device(cols, u_values, u_mask, p_values, p_mask, t_mask, out_mask):
    smem = pl.BlockSpec(memory_space=pltpu.SMEM)
    hbm = pl.BlockSpec(memory_space=pltpu.HBM)
    return pl.pallas_call(
        functools.partial(kernel, cols),
        out_shape=jax.ShapeDtypeStruct((2, 1, NO, B, B), F32),
        in_specs=[smem] * 4 + [hbm] * 2,
        out_specs=hbm,
        scratch_shapes=[
            pltpu.VMEM((12, 2, 4, B, B), F32),
            pltpu.VMEM((12, NO, B, B), F32),
            pltpu.VMEM((3, 16, B), F32),
            pltpu.VMEM((4, 4, B, B), F32),
            pltpu.VMEM((2, NO, B, B), F32),
            pltpu.VMEM((2, 16, B), F32),
            pltpu.VMEM((2 * B, 10 * B), F32),
            pltpu.VMEM((2 * B, 10 * B), BF16),
            pltpu.VMEM((2 * B, 10 * B), BF16),
            pltpu.VMEM((2, NO, B, B), F32),
            pltpu.SemaphoreType.DMA((COPIES,)),
            pltpu.SemaphoreType.DMA((COPIES,)),
            pltpu.SemaphoreType.DMA((COPIES,)),
            pltpu.SemaphoreType.DMA((8,)),
        ],
        compiler_params=pltpu.CompilerParams(
            collective_id=0, has_side_effects=True, vmem_limit_bytes=62 << 20),
        cost_estimate=pl.CostEstimate(
            flops=2 * 192 * B**3, bytes_accessed=3 << 20, transcendentals=0),
    )(
        u_mask.transpose(0, 2, 1), p_mask, t_mask.transpose(0, 2, 1), out_mask,
        u_values, p_values,
    )


def solution(mesh):
    placed = (
        P(("row", "col"), None, "layer", None, None),
        P(("row", "col"), None, "layer"),
        P(("row", "col"), "layer", None, None, None),
        P(("row", "col"), "layer", None),
        P(("row", "col"), None, "layer"),
        P(("row", "col"), "layer", None),
    )
    return jax.shard_map(
        functools.partial(on_device, mesh.shape["col"]),
        mesh=mesh,
        in_specs=placed,
        out_specs=P(("row", "col"), "layer", None, None, None),
        check_vma=False,
    )
```

```python
import functools

import jax
import jax.numpy as jnp
from jax import lax
from jax.experimental import pallas as pl
from jax.experimental.pallas import tpu as pltpu
from jax.sharding import PartitionSpec as P

B = 128
NO = 8
F32 = jnp.float32
BF16 = jnp.bfloat16
MESH = pl.DeviceIdType.MESH

S0_P, S0_U, S0_M = 0, 4, 8
S1_P, S1_U, S1_M = 9, 13, 17
H_P, H_UX, H_UY = 18, 24, 30
OUT = 36
STAND = 52
COPIES = 65
EARLY = 4
NATIVE = (
    "M A0 A1 Gp S4 S5 A2 A3 Gu S6 S7 "
    "t4 t6 A4 A5 t1 t9 ts tp1 tp3 t0 t8 t2 T "
    "A6 A7 o4 o6 oc2 oc3 os o1 o9 o0 o8 o2"
)
SWAPPED = (
    "S0 X S1 S2 S3 M A0 A1 S4 S5 A2 A3 S6 S7 "
    "t4 t6 t0 t8 t2 A4 A5 t1 t9 ts tp1 tp3 T "
    "o4 o6 A6 oc2 o0 o8 o2 A7 oc3 os o9 o1"
)
ORDER = [("p", 0), ("p", 1), ("p", 2), ("p", 3), ("u", 0), ("u", 1), ("u", 2), ("u", 3)]
STOOD = [("p", "s"), ("p", 1), ("p", 9), ("u", 2), ("u", 0), ("u", 8), ("u", "s"), ("u", 1), ("u", 9)]
X_AFTER = {("u", 0): (0, 8), ("u", 1): (2,), ("p", 3): ("s", 1, 9), ("u", 3): ("s", 1, 9)}
Y_AFTER = {("p", 1): (0, 8), ("p", 3): (2,), ("u", 1): ("s", 1, 9), ("u", 2): (0, 8), ("u", 3): (2,)}

REACH = {
    0: (True, 4, 4, 2, 2, 2, 2),
    1: (True, 3, 5, 2, 2, 1, 3),
    2: (True, 2, 6, 1, 3, 1, 3),
    8: (False, 0, 6, 0, 3, 0, 3),
    9: (False, 0, 5, 0, 3, 0, 2),
}
SLOT = {0: 0, 1: 1, 2: 2, 8: 3, 9: 4, "s": 5}


def split(x):
    high = x.astype(BF16)
    return high, (x - high.astype(F32)).astype(BF16)


def dot(a, b):
    return jnp.dot(a, b, preferred_element_type=F32)


def dot_t(a, b):
    return lax.dot_general(a, b, (((1,), (1,)), ((), ())), preferred_element_type=F32)


def kernel(cols, um, pm, tm, om, u_in, p_in, out, ub, pb, mb, su, sp, sm, t2, th, tl, ob,
           send, recv, local, load, far):
    core = lax.axis_index("row")
    col = lax.axis_index("col")
    layer = lax.axis_index("layer")
    half = col % 2
    quad = col // 2
    quads = cols // 2
    lam = (layer + core + half) % 2
    swaps = (core + half) % 2
    slabs = 4 * quads
    total = 4 * slabs
    first_row = 4 * (core * cols + col)

    def place(index):
        index = (index + slabs) % slabs
        h = index % 2
        q = index // 2
        p = q // quads
        return (h, (q % quads) * 2 + p, (1 - lam + h + p) % 2)

    chain = (half * quads + quad) * 2 + core
    up = place(chain + 1)
    down = place(chain - 1)
    partner = (core, col, 1 - layer)
    pair = (1 - core, quad * 2 + 1 - half, 1 - layer)

    def remote(src, dst, number, device):
        return pltpu.make_async_remote_copy(
            src_ref=src, dst_ref=dst, send_sem=send.at[number], recv_sem=recv.at[number],
            device_id=device, device_id_type=MESH)

    started = []

    def push(src, dst, number, device, ok=None):
        copy = remote(src, dst, number, device)
        started.append((copy, ok))
        if ok is None:
            copy.start()
        else:
            pl.when(ok)(copy.start)

    def got(view, number, ok=None):
        copy = remote(view, view, number, partner)
        if ok is None:
            copy.wait_recv()
        else:
            pl.when(ok)(copy.wait_recv)

    def keep(mask, index, column):
        ok = (column >= 0) & (column < total)
        return jnp.where(ok, mask[index], 0).astype(F32)

    last = quads - 1
    lower = chain != 0
    upper = chain != slabs - 1
    x_up = (core != 1) | (quad != last)
    x_down = (core != 0) | (quad != 0)
    stand_up = (swaps == 1) & (half == 1) & (quad == last)
    stand_down = (swaps == 1) & (half == 0) & (quad == 0)
    mate = (core, (last - quad) * 2 + half, layer)
    other_mate = (core, (last - quad) * 2 + half, 1 - layer)

    def p_chunk(cls, c):
        return pb.at[4 + cls + 2 * (c // 2), pl.ds(4 * (c % 2), 4)]

    def u_chunk(cls, c):
        row = [1 - cls, 3 - cls, cls, cls + 2][c]
        return ub.at[4 + row, [1, 1, 0, 0][c]]

    barrier = pltpu.get_barrier_semaphore()
    near_end = (swaps == 1) & (quad == 0)
    far_end = (swaps == 1) & (quad == last)
    far_down = near_end & (half == 1)
    far_up = far_end & (half == 0)

    def greet(device, ok=None):
        def signal():
            pl.semaphore_signal(barrier, inc=1, device_id=device, device_id_type=MESH)

        if ok is None:
            signal()
        else:
            pl.when(ok)(signal)

    greet(partner)
    greet(up, upper & ~far_up)
    greet(down, lower)
    greet(pair, swaps == 1)
    greet(mate, near_end)
    greet(other_mate, near_end)

    def p_stage(c):
        return sp.at[c // 2, pl.ds(4 * (c % 2), 4)]

    def u_row(c):
        return [1 - layer, 3 - layer, layer, layer + 2][c]

    def loads(c):
        yield pltpu.make_async_copy(
            p_in.at[c // 2, 0, pl.ds(4 * (c % 2), 4)], p_stage(c), load.at[c])
        yield pltpu.make_async_copy(
            u_in.at[u_row(c), pl.ds(0, 4), 0], su.at[c], load.at[4 + c])

    p_loads, u_loads = zip(*[tuple(loads(c)) for c in range(4)])
    for copy in p_loads + u_loads:
        copy.start()

    def stage_p(c, swap):
        a, o0 = c // 2, 4 * (c % 2)
        p_loads[c].wait()

        @pl.loop(0, 4)
        def _(s):
            column = first_row + layer + 2 * a - 4 + o0 + s
            value = sp[a, o0 + s] * keep(pm, (a, 0, o0 + s), column)
            if swap:
                sp[a, o0 + s] = value
            else:
                pb[4 + layer + 2 * a, o0 + s] = value

        if swap:
            push(p_stage(c), p_chunk(layer, c), S0_P + c, pair)

    def stage_u(c, swap):
        row = u_row(c)
        u_loads[c].wait()

        @pl.loop(0, 4)
        def _(s):
            column = first_row + row - 4 + [1, 1, 0, 0][c] + 2 * s
            value = su[c, s] * keep(um, (row, 0, s), column)
            if swap:
                su[c, s] = value
            else:
                ub[4 + row, [1, 1, 0, 0][c], s] = value

        if swap:
            push(su.at[c], u_chunk(layer, c), S0_U + c, pair)

    @pl.loop(0, 16)
    def _(s):
        row, m = s // 4, s % 4
        column = first_row + row - 4 + (layer + row) % 2 + 2 * m
        sm[0, pl.ds(s, 1), :] = jnp.full((1, B), keep(tm, (row, 0, m), column), F32)
        a, o = s // 8, s % 8
        column = first_row + layer + 2 * a - 4 + o
        sm[1, pl.ds(s, 1), :] = jnp.full((1, B), keep(om, (a, 0, o), column), F32)

    def clear(row):
        @pl.loop(row, row + 4)
        def _(r):
            @pl.loop(0, NO)
            def _(o):
                pb[r, o] = jnp.zeros((B, B), F32)
                ub[r, o // 4, o % 4] = jnp.zeros((B, B), F32)

    @pl.when(chain == 0)
    def _():
        clear(0)

    @pl.when(chain == slabs - 1)
    def _():
        clear(8)

    def may_send(key, cls):
        above, below = (x_up, x_down) if cls == "x" else (upper, lower)
        if key == "s":
            return ((lam == 1) & above) | ((lam == 0) & below)
        return above if REACH[key][0] else below

    def comes(key):
        if key == "s":
            return ((lam == 0) & lower) | ((lam == 1) & upper)
        return lower if REACH[key][0] else upper

    def stand_views(key, kind, cls):
        if key == "s":
            source, row = None, 8 - 5 * cls
        else:
            goes_up = REACH[key][0]
            source = key + 1 - cls if goes_up else key - 7 - cls
            row = source if goes_up else 8 + source
        if kind == "p":
            a = cls if key == "s" else 1 - cls
            blocks = pl.ds(cls, 7) if key == "s" else pl.ds(*REACH[key][1:3])
            return sp.at[a, blocks], pb.at[row, blocks], H_P + SLOT[key]
        c = {"s": 2 + cls, 0: 0, 8: 0, 2: 1, 1: 3 - cls, 9: 3 - cls}[key]
        parity = 0 if key == "s" else (key + 1) % 2
        slots = pl.ds(0, 4) if key == "s" else pl.ds(*u_slots(key, parity))
        return su.at[c, slots], ub.at[row, parity, slots], H_UX + SLOT[key]

    def stand_in(key, kind):
        source, target, number = stand_views(key, kind, layer)
        if key == "s":
            ok = (stand_up & (layer == 1)) | (stand_down & (layer == 0))
        else:
            ok = stand_up if REACH[key][0] else stand_down
        copy = pltpu.make_async_remote_copy(
            src_ref=source, dst_ref=target,
            send_sem=send.at[STAND + STOOD.index((kind, key))], recv_sem=recv.at[number],
            device_id=mate, device_id_type=MESH)
        pl.when(ok)(copy.start)
        started.append((copy, ok))

    def stand_in_y(key):
        goes_up = REACH[key][0]
        row = layer + (2 if key == 2 else 0)
        slots = pl.ds(*u_slots(key, 0))
        copy = pltpu.make_async_remote_copy(
            src_ref=su.at[3 if key == 2 else 2, slots],
            dst_ref=ub.at[row if goes_up else 8 + row, 0, slots],
            send_sem=send.at[STAND + len(STOOD) + SLOT[key]], recv_sem=recv.at[H_UY + SLOT[key]],
            device_id=other_mate, device_id_type=MESH)
        ok = stand_up if goes_up else stand_down
        pl.when(ok)(copy.start)
        started.append((copy, ok))

    def reach_p(key):
        if key == "s":
            push(pb.at[4 + 3 * lam, pl.ds(lam, 7)], pb.at[8 - 5 * lam, pl.ds(lam, 7)],
                 H_P + SLOT[key], special, may_send(key, "x"))
            return
        goes_up, o0, n = REACH[key][:3]
        row = key + 1 - lam if goes_up else key - 7 - lam
        push(pb.at[4 + row, pl.ds(o0, n)], pb.at[row if goes_up else 8 + row, pl.ds(o0, n)],
             H_P + SLOT[key], up if goes_up else down,
             may_send(key, "x" if key in (1, 9) else "y"))

    def got_p(key):
        if key == "s":
            got(pb.at[3 + 5 * lam, pl.ds(1 - lam, 7)], H_P + SLOT[key], comes(key))
            return
        _, o0, n = REACH[key][:3]
        got(pb.at[key + lam, pl.ds(o0, n)], H_P + SLOT[key], comes(key))

    def u_slots(key, parity):
        return REACH[key][3 + 2 * parity], REACH[key][4 + 2 * parity]

    def reach_u(key, cls):
        base = H_UX if cls == "x" else H_UY
        if key == "s":
            parity = 0 if cls == "x" else 1
            push(ub.at[4 + 3 * lam, parity], ub.at[8 - 5 * lam, parity],
                 base + SLOT[key], special, may_send(key, cls))
            return
        goes_up = REACH[key][0]
        parity = (key + 1) % 2 if cls == "x" else key % 2
        m0, n = u_slots(key, parity)
        row = key + 1 - lam if goes_up else key - 7 - lam
        push(ub.at[4 + row, parity, pl.ds(m0, n)],
             ub.at[row if goes_up else 8 + row, parity, pl.ds(m0, n)],
             base + SLOT[key], up if goes_up else down,
             may_send(key, "x" if key in (0, 8, 2) else cls))

    def got_u(key, classes=("x", "y")):
        for cls in classes:
            base = H_UX if cls == "x" else H_UY
            if key == "s":
                got(ub.at[3 + 5 * lam, 0 if cls == "x" else 1], base + SLOT[key], comes(key))
                continue
            parity = (key + 1) % 2 if cls == "x" else key % 2
            m0, n = u_slots(key, parity)
            got(ub.at[key + lam, parity, pl.ds(m0, n)], base + SLOT[key], comes(key))

    special = tuple(jnp.where(lam == 1, a, b) for a, b in zip(up, down))

    def t_step(k):
        lo, hi = max(0, k - 4), min(9, k + 3)
        width = hi - lo + 1
        rows = []
        if k < 8:
            rows.append(ub[4 + lam, k % 2, k // 2])
        if k >= 2:
            rows.append(ub[6 + lam, k % 2, (k - 2) // 2])
        a = rows[0] if len(rows) == 1 else jnp.concatenate(rows, axis=0)
        r0, r1 = (0 if k < 8 else B), (2 * B if k >= 2 else B)
        ah, al = split(a)
        both = jnp.concatenate([ah, al], axis=1)
        for w0 in range(0, width, 4):
            w1 = min(width, w0 + 4)
            b = jnp.concatenate(
                [pb[k + lam, lo + w - k + 4] for w in range(w0, w1)], axis=1)
            bh, bl = split(b)
            value = dot(both, jnp.concatenate([bh, bh], axis=0)) + dot(ah, bl)
            t2[r0:r1, (lo + w0) * B:(lo + w1) * B] += value

    def o_step(k, send_out):
        lo, hi = max(0, k - 4), min(9, k + 3)
        r0, r1 = (0 if k < 8 else B), (2 * B if k >= 2 else B)
        b = jnp.concatenate(
            [ub[lam + k, (j - k + 4) % 2, (j - k + 4) // 2] for j in range(lo, hi + 1)], axis=1)
        bh, bl = split(b)
        window = slice(lo * B, (hi + 1) * B)
        ah = th[r0:r1, window]
        value = dot_t(ah, bh) + dot_t(ah, bl) + dot_t(tl[r0:r1, window], bh)
        for a in range(2):
            o = k - 2 * a
            if 0 <= o < NO:
                block = value[a * B - r0:(a + 1) * B - r0]
                ob[a, o] = block * mb[1, pl.ds(a * 8 + o, 1), :]
                send_out(a, o)

    def finish_t():
        for a in range(2):
            for j in range(10):
                o = j - 2 * a
                spot = (slice(a * B, (a + 1) * B), slice(j * B, (j + 1) * B))
                if 0 <= o < NO:
                    row = (lam + 2 * a) * 4 + o // 2
                    value = t2[spot] * mb[0 if o % 2 == 0 else 2, pl.ds(row, 1), :]
                    high, low = split(value)
                else:
                    high = low = jnp.zeros((B, B), BF16)
                th[spot] = high
                tl[spot] = low

    def run(swap, early, steps):
        started.clear()
        seen = set()

        def swapped(n):
            kind, c = ORDER[n]
            if swap:
                if kind == "p":
                    got(p_chunk(lam, c), S0_P + c)
                else:
                    got(u_chunk(lam, c), S0_U + c)

        def send_on(n):
            kind, c = ORDER[n]
            swapped(n)
            view = (p_chunk if kind == "p" else u_chunk)(lam, c)
            push(view, view, (S1_P if kind == "p" else S1_U) + c, partner)
            for key in X_AFTER.get((kind, c), ()):
                (reach_p(key) if kind == "p" else reach_u(key, "x"))

        def arrived(n):
            kind, c = ORDER[n]
            got((p_chunk if kind == "p" else u_chunk)(1 - lam, c),
                (S1_P if kind == "p" else S1_U) + c)
            if swap and n == 1:
                pl.when(far_down)(lambda: pl.semaphore_wait(far, 1))
            for key in Y_AFTER.get((kind, c), ()):
                (reach_p(key) if kind == "p" else reach_u(key, "y"))

        def out_copy(a, o):
            view = out.at[a, 0, o]
            number = OUT + a * 8 + o
            if swap:
                return remote(ob.at[a, o], view, number, pair)
            return pltpu.make_async_copy(ob.at[a, o], view, local.at[number])

        def send_out(a, o):
            out_copy(a, o).start()

        def either(step, zero, one, *rest):
            pl.when(lam == 0)(lambda: step(zero, *rest))
            pl.when(lam == 1)(lambda: step(one, *rest))

        def o(key):
            if key == "s":
                got_u(key)
                either(o_step, 3, 7, send_out)
            elif key == "c2":
                either(o_step, 5, 3, send_out)
            elif key == "c3":
                either(o_step, 7, 5, send_out)
            else:
                if key in REACH:
                    got_u(key, ("y",) if key == 2 and "u" in seen else ("x", "y"))
                o_step(key, send_out)

        def t(key):
            if key == "s":
                got_p(key)
                either(t_step, 3, 7)
            elif key == "p1":
                either(t_step, 5, 3)
            elif key == "p3":
                either(t_step, 7, 5)
            else:
                if key in REACH and not (key == 1 and "p" in seen):
                    got_p(key)
                t_step(key)

        for n, (kind, c) in enumerate(ORDER):
            (stage_p if kind == "p" else stage_u)(c, swap)
            if n == 0:
                if swap:
                    push(sm, mb.at[pl.ds(0, 2)], S0_M, pair)
                else:
                    mb[0] = sm[0]
                    mb[1] = sm[1]
            if not swap and n < early:
                send_on(n)
        t2[...] = jnp.zeros_like(t2)
        for step in steps.split():
            what, key = step[0], step[1:]
            key = int(key) if key.isdigit() else key
            if what == "S":
                send_on(key)
            elif what == "A":
                arrived(key)
            elif what == "G":
                if key == "p":
                    got_p(1)
                else:
                    got_u(2, ("x",))
                seen.add(key)
            elif what == "X":
                pl.when(stand_down)(lambda: pl.semaphore_wait(far, 2))
                for kind, k in STOOD:
                    stand_in(k, kind)
                for k in (0, 8, 2):
                    stand_in_y(k)
            elif what == "M":
                if swap:
                    got(mb.at[pl.ds(0, 2)], S0_M)
                push(mb.at[0], mb.at[2], S1_M, partner)
            elif what == "t":
                t(key)
            elif what == "T":
                got(mb.at[2], S1_M)
                finish_t()
            else:
                o(key)

        for a in range(2):
            for p in range(NO):
                out_copy(a, p).wait()
        for copy, ok in started:
            if ok is None:
                copy.wait_send()
            else:
                pl.when(ok)(copy.wait_send)

    def count(ok):
        return ok.astype(jnp.int32)

    pl.semaphore_wait(
        barrier, 1 + swaps + count(upper) + count(lower & ~far_down) + 2 * count(far_end))

    @pl.when(far_up)
    def _():
        for device in (up, mate, other_mate):
            pl.semaphore_signal(far, inc=1, device_id=device, device_id_type=MESH)

    pl.when(swaps == 0)(lambda: run(False, EARLY, NATIVE))
    pl.when(swaps == 1)(lambda: run(True, 0, SWAPPED))


def on_device(cols, u_values, u_mask, p_values, p_mask, t_mask, out_mask):
    smem = pl.BlockSpec(memory_space=pltpu.SMEM)
    hbm = pl.BlockSpec(memory_space=pltpu.HBM)
    return pl.pallas_call(
        functools.partial(kernel, cols),
        out_shape=jax.ShapeDtypeStruct((2, 1, NO, B, B), F32),
        in_specs=[smem] * 4 + [hbm] * 2,
        out_specs=hbm,
        scratch_shapes=[
            pltpu.VMEM((12, 2, 4, B, B), F32),
            pltpu.VMEM((12, NO, B, B), F32),
            pltpu.VMEM((3, 16, B), F32),
            pltpu.VMEM((4, 4, B, B), F32),
            pltpu.VMEM((2, NO, B, B), F32),
            pltpu.VMEM((2, 16, B), F32),
            pltpu.VMEM((2 * B, 10 * B), F32),
            pltpu.VMEM((2 * B, 10 * B), BF16),
            pltpu.VMEM((2 * B, 10 * B), BF16),
            pltpu.VMEM((2, NO, B, B), F32),
            pltpu.SemaphoreType.DMA((COPIES,)),
            pltpu.SemaphoreType.DMA((COPIES,)),
            pltpu.SemaphoreType.DMA((COPIES,)),
            pltpu.SemaphoreType.DMA((8,)),
            pltpu.SemaphoreType.REGULAR,
        ],
        compiler_params=pltpu.CompilerParams(
            collective_id=0, has_side_effects=True, vmem_limit_bytes=62 << 20),
        cost_estimate=pl.CostEstimate(
            flops=2 * 192 * B**3, bytes_accessed=3 << 20, transcendentals=0),
    )(
        u_mask.transpose(0, 2, 1), p_mask, t_mask.transpose(0, 2, 1), out_mask,
        u_values, p_values,
    )


def solution(mesh):
    placed = (
        P(("row", "col"), None, "layer", None, None),
        P(("row", "col"), None, "layer"),
        P(("row", "col"), "layer", None, None, None),
        P(("row", "col"), "layer", None),
        P(("row", "col"), None, "layer"),
        P(("row", "col"), "layer", None),
    )
    return jax.shard_map(
        functools.partial(on_device, mesh.shape["col"]),
        mesh=mesh,
        in_specs=placed,
        out_specs=P(("row", "col"), "layer", None, None, None),
        check_vma=False,
    )
```

```python
import functools

import jax
import jax.numpy as jnp
from jax import lax
from jax.experimental import pallas as pl
from jax.experimental.pallas import tpu as pltpu
from jax.sharding import PartitionSpec as P

B = 128
NO = 8
F32 = jnp.float32
BF16 = jnp.bfloat16
MESH = pl.DeviceIdType.MESH

S0_P, S0_U, S0_M = 0, 4, 8
S1_P, S1_U, S1_M = 9, 13, 17
H_P, H_UX, H_UY = 18, 24, 30
OUT = 36
STAND = 52
COPIES = 65
EARLY = 4
NATIVE = [
    "M", "A0", "A1", "Gp", "S4", "S5", "A2", "A3", "Gu", "S6", "S7", "t4", "t6", "A4", "A5",
    "t1", "t9", "ts", "tp1", "tp3", "t0", "t8", "t2", "T", "A6", "A7", "o4", "o6", "oc2", "oc3",
    "os", "o1", "o9", "o0", "o8", "o2",
]
SWAPPED = [
    "S0", "X", "S1", "S2", "S3", "M", "A0", "A1", "S4", "S5", "A2", "A3", "S6", "S7", "t4",
    "t6", "t0", "t8", "t2", "A4", "A5", "t1", "t9", "ts", "tp1", "tp3", "T", "o4", "o6", "A6",
    "oc2", "o0", "o8", "o2", "A7", "oc3", "os", "o9", "o1",
]
INNER = [
    "o4", "o6", "os", "A6", "oc2", "o9", "o1", "o0", "o8", "A7", "oc3", "o2",
]
ORDER = [("p", 0), ("p", 1), ("p", 2), ("p", 3), ("u", 0), ("u", 1), ("u", 2), ("u", 3)]
STOOD = [("p", "s"), ("p", 1), ("p", 9), ("u", 2), ("u", 0), ("u", 8), ("u", "s"), ("u", 1), ("u", 9)]
X_AFTER = {("u", 0): (0, 8), ("u", 1): (2,), ("p", 3): ("s", 1, 9), ("u", 3): ("s", 1, 9)}
Y_AFTER = {("p", 1): (0, 8), ("p", 3): (2,), ("u", 1): ("s", 1, 9), ("u", 2): (0, 8), ("u", 3): (2,)}

REACH = {
    0: (True, 4, 4, 2, 2, 2, 2),
    1: (True, 3, 5, 2, 2, 1, 3),
    2: (True, 2, 6, 1, 3, 1, 3),
    8: (False, 0, 6, 0, 3, 0, 3),
    9: (False, 0, 5, 0, 3, 0, 2),
}
SLOT = {0: 0, 1: 1, 2: 2, 8: 3, 9: 4, "s": 5}


def split(x):
    high = x.astype(BF16)
    return high, (x - high.astype(F32)).astype(BF16)


def dot(a, b):
    return jnp.dot(a, b, preferred_element_type=F32)


def dot_t(a, b):
    return lax.dot_general(a, b, (((1,), (1,)), ((), ())), preferred_element_type=F32)


def kernel(cols, um, pm, tm, om, u_in, p_in, out, ub, pb, mb, su, sp, sm, t2, th, tl, ob,
           send, recv, local, load, far):
    core = lax.axis_index("row")
    col = lax.axis_index("col")
    layer = lax.axis_index("layer")
    half = col % 2
    quad = col // 2
    quads = cols // 2
    lam = (layer + core + half) % 2
    swaps = (core + half) % 2
    slabs = 4 * quads
    total = 4 * slabs
    first_row = 4 * (core * cols + col)

    def place(index):
        index = (index + slabs) % slabs
        h = index % 2
        q = index // 2
        p = q // quads
        return (h, (q % quads) * 2 + p, (1 - lam + h + p) % 2)

    chain = (half * quads + quad) * 2 + core
    up = place(chain + 1)
    down = place(chain - 1)
    partner = (core, col, 1 - layer)
    pair = (1 - core, quad * 2 + 1 - half, 1 - layer)

    def remote(src, dst, number, device):
        return pltpu.make_async_remote_copy(
            src_ref=src, dst_ref=dst, send_sem=send.at[number], recv_sem=recv.at[number],
            device_id=device, device_id_type=MESH)

    started = []

    def push(src, dst, number, device, ok=None):
        copy = remote(src, dst, number, device)
        started.append((copy, ok))
        if ok is None:
            copy.start()
        else:
            pl.when(ok)(copy.start)

    def got(view, number, ok=None):
        copy = remote(view, view, number, partner)
        if ok is None:
            copy.wait_recv()
        else:
            pl.when(ok)(copy.wait_recv)

    def keep(mask, index, column):
        ok = (column >= 0) & (column < total)
        return jnp.where(ok, mask[index], 0).astype(F32)

    last = quads - 1
    lower = chain != 0
    upper = chain != slabs - 1
    x_up = (core != 1) | (quad != last)
    x_down = (core != 0) | (quad != 0)
    stand_up = (swaps == 1) & (half == 1) & (quad == last)
    stand_down = (swaps == 1) & (half == 0) & (quad == 0)
    mate = (core, (last - quad) * 2 + half, layer)
    other_mate = (core, (last - quad) * 2 + half, 1 - layer)

    def p_chunk(cls, c):
        return pb.at[4 + cls + 2 * (c // 2), pl.ds(4 * (c % 2), 4)]

    def u_chunk(cls, c):
        row = [1 - cls, 3 - cls, cls, cls + 2][c]
        return ub.at[4 + row, [1, 1, 0, 0][c]]

    barrier = pltpu.get_barrier_semaphore()
    near_end = (swaps == 1) & (quad == 0)
    far_end = (swaps == 1) & (quad == last)
    far_down = near_end & (half == 1)
    far_up = far_end & (half == 0)

    def greet(device, ok=None):
        def signal():
            pl.semaphore_signal(barrier, inc=1, device_id=device, device_id_type=MESH)

        if ok is None:
            signal()
        else:
            pl.when(ok)(signal)

    greet(partner)
    greet(up, upper & ~far_up)
    greet(down, lower)
    greet(pair, swaps == 1)
    greet(mate, near_end)
    greet(other_mate, near_end)

    def p_stage(c):
        return sp.at[c // 2, pl.ds(4 * (c % 2), 4)]

    def u_row(c):
        return [1 - layer, 3 - layer, layer, layer + 2][c]

    def loads(c):
        yield pltpu.make_async_copy(
            p_in.at[c // 2, 0, pl.ds(4 * (c % 2), 4)], p_stage(c), load.at[c])
        yield pltpu.make_async_copy(
            u_in.at[u_row(c), pl.ds(0, 4), 0], su.at[c], load.at[4 + c])

    p_loads, u_loads = zip(*[tuple(loads(c)) for c in range(4)])
    for copy in p_loads + u_loads:
        copy.start()

    def stage_p(c, swap):
        a, o0 = c // 2, 4 * (c % 2)
        p_loads[c].wait()

        @pl.loop(0, 4)
        def _(s):
            column = first_row + layer + 2 * a - 4 + o0 + s
            value = sp[a, o0 + s] * keep(pm, (a, 0, o0 + s), column)
            if swap:
                sp[a, o0 + s] = value
            else:
                pb[4 + layer + 2 * a, o0 + s] = value

        if swap:
            push(p_stage(c), p_chunk(layer, c), S0_P + c, pair)

    def stage_u(c, swap):
        row = u_row(c)
        u_loads[c].wait()

        @pl.loop(0, 4)
        def _(s):
            column = first_row + row - 4 + [1, 1, 0, 0][c] + 2 * s
            value = su[c, s] * keep(um, (row, 0, s), column)
            if swap:
                su[c, s] = value
            else:
                ub[4 + row, [1, 1, 0, 0][c], s] = value

        if swap:
            push(su.at[c], u_chunk(layer, c), S0_U + c, pair)

    @pl.loop(0, 16)
    def _(s):
        row, m = s // 4, s % 4
        column = first_row + row - 4 + (layer + row) % 2 + 2 * m
        sm[0, pl.ds(s, 1), :] = jnp.full((1, B), keep(tm, (row, 0, m), column), F32)
        a, o = s // 8, s % 8
        column = first_row + layer + 2 * a - 4 + o
        sm[1, pl.ds(s, 1), :] = jnp.full((1, B), keep(om, (a, 0, o), column), F32)

    def clear(row):
        @pl.loop(row, row + 4)
        def _(r):
            @pl.loop(0, NO)
            def _(o):
                pb[r, o] = jnp.zeros((B, B), F32)
                ub[r, o // 4, o % 4] = jnp.zeros((B, B), F32)

    @pl.when(chain == 0)
    def _():
        clear(0)

    @pl.when(chain == slabs - 1)
    def _():
        clear(8)

    def may_send(key, cls):
        above, below = (x_up, x_down) if cls == "x" else (upper, lower)
        if key == "s":
            return ((lam == 1) & above) | ((lam == 0) & below)
        return above if REACH[key][0] else below

    def comes(key):
        if key == "s":
            return ((lam == 0) & lower) | ((lam == 1) & upper)
        return lower if REACH[key][0] else upper

    def stand_views(key, kind, cls):
        if key == "s":
            source, row = None, 8 - 5 * cls
        else:
            goes_up = REACH[key][0]
            source = key + 1 - cls if goes_up else key - 7 - cls
            row = source if goes_up else 8 + source
        if kind == "p":
            a = cls if key == "s" else 1 - cls
            blocks = pl.ds(cls, 7) if key == "s" else pl.ds(*REACH[key][1:3])
            return sp.at[a, blocks], pb.at[row, blocks], H_P + SLOT[key]
        c = {"s": 2 + cls, 0: 0, 8: 0, 2: 1, 1: 3 - cls, 9: 3 - cls}[key]
        parity = 0 if key == "s" else (key + 1) % 2
        slots = pl.ds(0, 4) if key == "s" else pl.ds(*u_slots(key, parity))
        return su.at[c, slots], ub.at[row, parity, slots], H_UX + SLOT[key]

    def stand_in(key, kind):
        source, target, number = stand_views(key, kind, layer)
        if key == "s":
            ok = (stand_up & (layer == 1)) | (stand_down & (layer == 0))
        else:
            ok = stand_up if REACH[key][0] else stand_down
        copy = pltpu.make_async_remote_copy(
            src_ref=source, dst_ref=target,
            send_sem=send.at[STAND + STOOD.index((kind, key))], recv_sem=recv.at[number],
            device_id=mate, device_id_type=MESH)
        pl.when(ok)(copy.start)
        started.append((copy, ok))

    def stand_in_y(key):
        goes_up = REACH[key][0]
        row = layer + (2 if key == 2 else 0)
        slots = pl.ds(*u_slots(key, 0))
        copy = pltpu.make_async_remote_copy(
            src_ref=su.at[3 if key == 2 else 2, slots],
            dst_ref=ub.at[row if goes_up else 8 + row, 0, slots],
            send_sem=send.at[STAND + len(STOOD) + SLOT[key]], recv_sem=recv.at[H_UY + SLOT[key]],
            device_id=other_mate, device_id_type=MESH)
        ok = stand_up if goes_up else stand_down
        pl.when(ok)(copy.start)
        started.append((copy, ok))

    def reach_p(key):
        if key == "s":
            push(pb.at[4 + 3 * lam, pl.ds(lam, 7)], pb.at[8 - 5 * lam, pl.ds(lam, 7)],
                 H_P + SLOT[key], special, may_send(key, "x"))
            return
        goes_up, o0, n = REACH[key][:3]
        row = key + 1 - lam if goes_up else key - 7 - lam
        push(pb.at[4 + row, pl.ds(o0, n)], pb.at[row if goes_up else 8 + row, pl.ds(o0, n)],
             H_P + SLOT[key], up if goes_up else down,
             may_send(key, "x" if key in (1, 9) else "y"))

    def got_p(key):
        if key == "s":
            got(pb.at[3 + 5 * lam, pl.ds(1 - lam, 7)], H_P + SLOT[key], comes(key))
            return
        _, o0, n = REACH[key][:3]
        got(pb.at[key + lam, pl.ds(o0, n)], H_P + SLOT[key], comes(key))

    def u_slots(key, parity):
        return REACH[key][3 + 2 * parity], REACH[key][4 + 2 * parity]

    def reach_u(key, cls):
        base = H_UX if cls == "x" else H_UY
        if key == "s":
            parity = 0 if cls == "x" else 1
            push(ub.at[4 + 3 * lam, parity], ub.at[8 - 5 * lam, parity],
                 base + SLOT[key], special, may_send(key, cls))
            return
        goes_up = REACH[key][0]
        parity = (key + 1) % 2 if cls == "x" else key % 2
        m0, n = u_slots(key, parity)
        row = key + 1 - lam if goes_up else key - 7 - lam
        push(ub.at[4 + row, parity, pl.ds(m0, n)],
             ub.at[row if goes_up else 8 + row, parity, pl.ds(m0, n)],
             base + SLOT[key], up if goes_up else down,
             may_send(key, "x" if key in (0, 8, 2) else cls))

    def got_u(key, classes=("x", "y")):
        for cls in classes:
            base = H_UX if cls == "x" else H_UY
            if key == "s":
                got(ub.at[3 + 5 * lam, 0 if cls == "x" else 1], base + SLOT[key], comes(key))
                continue
            parity = (key + 1) % 2 if cls == "x" else key % 2
            m0, n = u_slots(key, parity)
            got(ub.at[key + lam, parity, pl.ds(m0, n)], base + SLOT[key], comes(key))

    special = tuple(jnp.where(lam == 1, a, b) for a, b in zip(up, down))

    def t_step(k):
        lo, hi = max(0, k - 4), min(9, k + 3)
        width = hi - lo + 1
        rows = []
        if k < 8:
            rows.append(ub[4 + lam, k % 2, k // 2])
        if k >= 2:
            rows.append(ub[6 + lam, k % 2, (k - 2) // 2])
        a = rows[0] if len(rows) == 1 else jnp.concatenate(rows, axis=0)
        r0, r1 = (0 if k < 8 else B), (2 * B if k >= 2 else B)
        ah, al = split(a)
        both = jnp.concatenate([ah, al], axis=1)
        for w0 in range(0, width, 4):
            w1 = min(width, w0 + 4)
            b = jnp.concatenate(
                [pb[k + lam, lo + w - k + 4] for w in range(w0, w1)], axis=1)
            bh, bl = split(b)
            value = dot(both, jnp.concatenate([bh, bh], axis=0)) + dot(ah, bl)
            t2[r0:r1, (lo + w0) * B:(lo + w1) * B] += value

    def o_step(k, send_out):
        lo, hi = max(0, k - 4), min(9, k + 3)
        r0, r1 = (0 if k < 8 else B), (2 * B if k >= 2 else B)
        b = jnp.concatenate(
            [ub[lam + k, (j - k + 4) % 2, (j - k + 4) // 2] for j in range(lo, hi + 1)], axis=1)
        bh, bl = split(b)
        window = slice(lo * B, (hi + 1) * B)
        ah = th[r0:r1, window]
        value = dot_t(ah, bh) + dot_t(ah, bl) + dot_t(tl[r0:r1, window], bh)
        for a in range(2):
            o = k - 2 * a
            if 0 <= o < NO:
                block = value[a * B - r0:(a + 1) * B - r0]
                ob[a, o] = block * mb[1, pl.ds(a * 8 + o, 1), :]
                send_out(a, o)

    def finish_t():
        for a in range(2):
            for j in range(10):
                o = j - 2 * a
                spot = (slice(a * B, (a + 1) * B), slice(j * B, (j + 1) * B))
                if 0 <= o < NO:
                    row = (lam + 2 * a) * 4 + o // 2
                    value = t2[spot] * mb[0 if o % 2 == 0 else 2, pl.ds(row, 1), :]
                    high, low = split(value)
                else:
                    high = low = jnp.zeros((B, B), BF16)
                th[spot] = high
                tl[spot] = low

    def run(swap, early, steps, at_end=True):
        started.clear()
        seen = set()

        def swapped(n):
            kind, c = ORDER[n]
            if swap:
                if kind == "p":
                    got(p_chunk(lam, c), S0_P + c)
                else:
                    got(u_chunk(lam, c), S0_U + c)

        def send_on(n):
            kind, c = ORDER[n]
            swapped(n)
            view = (p_chunk if kind == "p" else u_chunk)(lam, c)
            push(view, view, (S1_P if kind == "p" else S1_U) + c, partner)
            for key in X_AFTER.get((kind, c), ()):
                (reach_p(key) if kind == "p" else reach_u(key, "x"))

        def arrived(n):
            kind, c = ORDER[n]
            got((p_chunk if kind == "p" else u_chunk)(1 - lam, c),
                (S1_P if kind == "p" else S1_U) + c)
            if swap and n == 1:
                pl.when(far_down)(lambda: pl.semaphore_wait(far, 1))
            for key in Y_AFTER.get((kind, c), ()):
                (reach_p(key) if kind == "p" else reach_u(key, "y"))

        def out_copy(a, o):
            view = out.at[a, 0, o]
            number = OUT + a * 8 + o
            if swap:
                return remote(ob.at[a, o], view, number, pair)
            return pltpu.make_async_copy(ob.at[a, o], view, local.at[number])

        def send_out(a, o):
            out_copy(a, o).start()

        def either(step, zero, one, *rest):
            pl.when(lam == 0)(lambda: step(zero, *rest))
            pl.when(lam == 1)(lambda: step(one, *rest))

        def o(key):
            if key == "s":
                got_u(key)
                either(o_step, 3, 7, send_out)
            elif key == "c2":
                either(o_step, 5, 3, send_out)
            elif key == "c3":
                either(o_step, 7, 5, send_out)
            else:
                if key in REACH:
                    got_u(key, ("y",) if key == 2 and "u" in seen else ("x", "y"))
                o_step(key, send_out)

        def t(key):
            if key == "s":
                got_p(key)
                either(t_step, 3, 7)
            elif key == "p1":
                either(t_step, 5, 3)
            elif key == "p3":
                either(t_step, 7, 5)
            else:
                if key in REACH and not (key == 1 and "p" in seen):
                    got_p(key)
                t_step(key)

        for n, (kind, c) in enumerate(ORDER):
            (stage_p if kind == "p" else stage_u)(c, swap)
            if n == 0:
                if swap:
                    push(sm, mb.at[pl.ds(0, 2)], S0_M, pair)
                else:
                    mb[0] = sm[0]
                    mb[1] = sm[1]
            if not swap and n < early:
                send_on(n)
        t2[...] = jnp.zeros_like(t2)
        for step in steps:
            what, key = step[0], step[1:]
            key = int(key) if key.isdigit() else key
            if what == "S":
                send_on(key)
            elif what == "A":
                arrived(key)
            elif what == "G":
                if key == "p":
                    got_p(1)
                else:
                    got_u(2, ("x",))
                seen.add(key)
            elif what == "X" and at_end:
                pl.when(stand_down)(lambda: pl.semaphore_wait(far, 2))
                for kind, k in STOOD:
                    stand_in(k, kind)
                for k in (0, 8, 2):
                    stand_in_y(k)
            elif what == "X":
                pass
            elif what == "M":
                if swap:
                    got(mb.at[pl.ds(0, 2)], S0_M)
                push(mb.at[0], mb.at[2], S1_M, partner)
            elif what == "t":
                t(key)
            elif what == "T":
                got(mb.at[2], S1_M)
                finish_t()
            else:
                o(key)

        for a in range(2):
            for p in range(NO):
                out_copy(a, p).wait()
        for copy, ok in started:
            if ok is None:
                copy.wait_send()
            else:
                pl.when(ok)(copy.wait_send)

    def count(ok):
        return ok.astype(jnp.int32)

    pl.semaphore_wait(
        barrier, 1 + swaps + count(upper) + count(lower & ~far_down) + 2 * count(far_end))

    @pl.when(far_up)
    def _():
        for device in (up, mate, other_mate):
            pl.semaphore_signal(far, inc=1, device_id=device, device_id_type=MESH)

    pl.when(swaps == 0)(lambda: run(False, EARLY, NATIVE))
    ends = near_end | far_end
    pl.when((swaps == 1) & ~ends)(lambda: run(True, 0, SWAPPED[:-12] + INNER, False))
    pl.when((swaps == 1) & ends)(lambda: run(True, 0, SWAPPED))


def on_device(cols, u_values, u_mask, p_values, p_mask, t_mask, out_mask):
    smem = pl.BlockSpec(memory_space=pltpu.SMEM)
    hbm = pl.BlockSpec(memory_space=pltpu.HBM)
    return pl.pallas_call(
        functools.partial(kernel, cols),
        out_shape=jax.ShapeDtypeStruct((2, 1, NO, B, B), F32),
        in_specs=[smem] * 4 + [hbm] * 2,
        out_specs=hbm,
        scratch_shapes=[
            pltpu.VMEM((12, 2, 4, B, B), F32),
            pltpu.VMEM((12, NO, B, B), F32),
            pltpu.VMEM((3, 16, B), F32),
            pltpu.VMEM((4, 4, B, B), F32),
            pltpu.VMEM((2, NO, B, B), F32),
            pltpu.VMEM((2, 16, B), F32),
            pltpu.VMEM((2 * B, 10 * B), F32),
            pltpu.VMEM((2 * B, 10 * B), BF16),
            pltpu.VMEM((2 * B, 10 * B), BF16),
            pltpu.VMEM((2, NO, B, B), F32),
            pltpu.SemaphoreType.DMA((COPIES,)),
            pltpu.SemaphoreType.DMA((COPIES,)),
            pltpu.SemaphoreType.DMA((COPIES,)),
            pltpu.SemaphoreType.DMA((8,)),
            pltpu.SemaphoreType.REGULAR,
        ],
        compiler_params=pltpu.CompilerParams(
            collective_id=0, has_side_effects=True, vmem_limit_bytes=62 << 20),
        cost_estimate=pl.CostEstimate(
            flops=2 * 192 * B**3, bytes_accessed=3 << 20, transcendentals=0),
    )(
        u_mask.transpose(0, 2, 1), p_mask, t_mask.transpose(0, 2, 1), out_mask,
        u_values, p_values,
    )


def solution(mesh):
    placed = (
        P(("row", "col"), None, "layer", None, None),
        P(("row", "col"), None, "layer"),
        P(("row", "col"), "layer", None, None, None),
        P(("row", "col"), "layer", None),
        P(("row", "col"), None, "layer"),
        P(("row", "col"), "layer", None),
    )
    return jax.shard_map(
        functools.partial(on_device, mesh.shape["col"]),
        mesh=mesh,
        in_specs=placed,
        out_specs=P(("row", "col"), "layer", None, None, None),
        check_vma=False,
    )
```

```python
import functools

import jax
import jax.numpy as jnp
from jax import lax
from jax.experimental import pallas as pl
from jax.experimental.pallas import tpu as pltpu
from jax.sharding import PartitionSpec as P

B = 128
NO = 8
F32 = jnp.float32
BF16 = jnp.bfloat16
MESH = pl.DeviceIdType.MESH

S0_P, S0_U, S0_M = 0, 4, 8
S1_P, S1_U, S1_M = 9, 13, 17
H_P, H_UX, H_UY = 18, 24, 30
OUT = 36
STAND = 52
COPIES = 65
EARLY = 4
NATIVE = [
    "M", "A0", "A1", "Gp", "S4", "S5", "A2", "A3", "Gu", "S6", "S7", "t4", "t6", "A4", "A5",
    "t1", "t9", "ts", "tp1", "tp3", "t0", "t8", "t2", "T", "A6", "A7", "o4", "o6", "oc2", "oc3",
    "os", "o1", "o9", "o0", "o8", "o2",
]
SWAPPED = [
    "S0", "X", "S1", "S2", "S3", "M", "A0", "A1", "S4", "S5", "A2", "A3", "S6", "S7", "t4",
    "t6", "t0", "t8", "t2", "A4", "t1", "xs", "xp1", "xp3", "V", "A5", "ys", "yp1", "yp3", "t9",
    "W", "o4", "o6", "A6", "oc2", "o0", "o8", "o2", "A7", "oc3", "os", "o9", "o1",
]
INNER = [
    "o4", "o6", "os", "A6", "oc2", "o9", "o1", "o0", "o8", "A7", "oc3", "o2",
]
ORDER = [("p", 0), ("p", 1), ("p", 2), ("p", 3), ("u", 0), ("u", 1), ("u", 2), ("u", 3)]
STOOD = [("p", "s"), ("p", 1), ("p", 9), ("u", 2), ("u", 0), ("u", 8), ("u", "s"), ("u", 1), ("u", 9)]
X_AFTER = {("u", 0): (0, 8), ("u", 1): (2,), ("p", 3): ("s", 1, 9), ("u", 3): ("s", 1, 9)}
Y_AFTER = {("p", 1): (0, 8), ("p", 3): (2,), ("u", 1): ("s", 1, 9), ("u", 2): (0, 8), ("u", 3): (2,)}

REACH = {
    0: (True, 4, 4, 2, 2, 2, 2),
    1: (True, 3, 5, 2, 2, 1, 3),
    2: (True, 2, 6, 1, 3, 1, 3),
    8: (False, 0, 6, 0, 3, 0, 3),
    9: (False, 0, 5, 0, 3, 0, 2),
}
EITHER = {"s": (3, 7), "p1": (5, 3), "p3": (7, 5)}
SLOT = {0: 0, 1: 1, 2: 2, 8: 3, 9: 4, "s": 5}


def split(x):
    high = x.astype(BF16)
    return high, (x - high.astype(F32)).astype(BF16)


def dot(a, b):
    return jnp.dot(a, b, preferred_element_type=F32)


def dot_t(a, b):
    return lax.dot_general(a, b, (((1,), (1,)), ((), ())), preferred_element_type=F32)


def kernel(cols, um, pm, tm, om, u_in, p_in, out, ub, pb, mb, su, sp, sm, t2, th, tl, ob,
           send, recv, local, load, far):
    core = lax.axis_index("row")
    col = lax.axis_index("col")
    layer = lax.axis_index("layer")
    half = col % 2
    quad = col // 2
    quads = cols // 2
    lam = (layer + core + half) % 2
    swaps = (core + half) % 2
    slabs = 4 * quads
    total = 4 * slabs
    first_row = 4 * (core * cols + col)

    def place(index):
        index = (index + slabs) % slabs
        h = index % 2
        q = index // 2
        p = q // quads
        return (h, (q % quads) * 2 + p, (1 - lam + h + p) % 2)

    chain = (half * quads + quad) * 2 + core
    up = place(chain + 1)
    down = place(chain - 1)
    partner = (core, col, 1 - layer)
    pair = (1 - core, quad * 2 + 1 - half, 1 - layer)

    def remote(src, dst, number, device):
        return pltpu.make_async_remote_copy(
            src_ref=src, dst_ref=dst, send_sem=send.at[number], recv_sem=recv.at[number],
            device_id=device, device_id_type=MESH)

    started = []

    def push(src, dst, number, device, ok=None):
        copy = remote(src, dst, number, device)
        started.append((copy, ok))
        if ok is None:
            copy.start()
        else:
            pl.when(ok)(copy.start)

    def got(view, number, ok=None):
        copy = remote(view, view, number, partner)
        if ok is None:
            copy.wait_recv()
        else:
            pl.when(ok)(copy.wait_recv)

    def keep(mask, index, column):
        ok = (column >= 0) & (column < total)
        return jnp.where(ok, mask[index], 0).astype(F32)

    last = quads - 1
    lower = chain != 0
    upper = chain != slabs - 1
    x_up = (core != 1) | (quad != last)
    x_down = (core != 0) | (quad != 0)
    stand_up = (swaps == 1) & (half == 1) & (quad == last)
    stand_down = (swaps == 1) & (half == 0) & (quad == 0)
    mate = (core, (last - quad) * 2 + half, layer)
    other_mate = (core, (last - quad) * 2 + half, 1 - layer)

    def p_chunk(cls, c):
        return pb.at[4 + cls + 2 * (c // 2), pl.ds(4 * (c % 2), 4)]

    def u_chunk(cls, c):
        row = [1 - cls, 3 - cls, cls, cls + 2][c]
        return ub.at[4 + row, [1, 1, 0, 0][c]]

    barrier = pltpu.get_barrier_semaphore()
    near_end = (swaps == 1) & (quad == 0)
    far_end = (swaps == 1) & (quad == last)
    far_down = near_end & (half == 1)
    far_up = far_end & (half == 0)

    def greet(device, ok=None):
        def signal():
            pl.semaphore_signal(barrier, inc=1, device_id=device, device_id_type=MESH)

        if ok is None:
            signal()
        else:
            pl.when(ok)(signal)

    greet(partner)
    greet(up, upper & ~far_up)
    greet(down, lower)
    greet(pair, swaps == 1)
    greet(mate, near_end)
    greet(other_mate, near_end)

    def p_stage(c):
        return sp.at[c // 2, pl.ds(4 * (c % 2), 4)]

    def u_row(c):
        return [1 - layer, 3 - layer, layer, layer + 2][c]

    def loads(c):
        yield pltpu.make_async_copy(
            p_in.at[c // 2, 0, pl.ds(4 * (c % 2), 4)], p_stage(c), load.at[c])
        yield pltpu.make_async_copy(
            u_in.at[u_row(c), pl.ds(0, 4), 0], su.at[c], load.at[4 + c])

    p_loads, u_loads = zip(*[tuple(loads(c)) for c in range(4)])
    for copy in p_loads + u_loads:
        copy.start()

    def stage_p(c, swap):
        a, o0 = c // 2, 4 * (c % 2)
        p_loads[c].wait()

        @pl.loop(0, 4)
        def _(s):
            column = first_row + layer + 2 * a - 4 + o0 + s
            value = sp[a, o0 + s] * keep(pm, (a, 0, o0 + s), column)
            if swap:
                sp[a, o0 + s] = value
            else:
                pb[4 + layer + 2 * a, o0 + s] = value

        if swap:
            push(p_stage(c), p_chunk(layer, c), S0_P + c, pair)

    def stage_u(c, swap):
        row = u_row(c)
        u_loads[c].wait()

        @pl.loop(0, 4)
        def _(s):
            column = first_row + row - 4 + [1, 1, 0, 0][c] + 2 * s
            value = su[c, s] * keep(um, (row, 0, s), column)
            if swap:
                su[c, s] = value
            else:
                ub[4 + row, [1, 1, 0, 0][c], s] = value

        if swap:
            push(su.at[c], u_chunk(layer, c), S0_U + c, pair)

    @pl.loop(0, 16)
    def _(s):
        row, m = s // 4, s % 4
        column = first_row + row - 4 + (layer + row) % 2 + 2 * m
        sm[0, pl.ds(s, 1), :] = jnp.full((1, B), keep(tm, (row, 0, m), column), F32)
        a, o = s // 8, s % 8
        column = first_row + layer + 2 * a - 4 + o
        sm[1, pl.ds(s, 1), :] = jnp.full((1, B), keep(om, (a, 0, o), column), F32)

    def clear(row):
        @pl.loop(row, row + 4)
        def _(r):
            @pl.loop(0, NO)
            def _(o):
                pb[r, o] = jnp.zeros((B, B), F32)
                ub[r, o // 4, o % 4] = jnp.zeros((B, B), F32)

    @pl.when(chain == 0)
    def _():
        clear(0)

    @pl.when(chain == slabs - 1)
    def _():
        clear(8)

    def may_send(key, cls):
        above, below = (x_up, x_down) if cls == "x" else (upper, lower)
        if key == "s":
            return ((lam == 1) & above) | ((lam == 0) & below)
        return above if REACH[key][0] else below

    def comes(key):
        if key == "s":
            return ((lam == 0) & lower) | ((lam == 1) & upper)
        return lower if REACH[key][0] else upper

    def stand_views(key, kind, cls):
        if key == "s":
            source, row = None, 8 - 5 * cls
        else:
            goes_up = REACH[key][0]
            source = key + 1 - cls if goes_up else key - 7 - cls
            row = source if goes_up else 8 + source
        if kind == "p":
            a = cls if key == "s" else 1 - cls
            blocks = pl.ds(cls, 7) if key == "s" else pl.ds(*REACH[key][1:3])
            return sp.at[a, blocks], pb.at[row, blocks], H_P + SLOT[key]
        c = {"s": 2 + cls, 0: 0, 8: 0, 2: 1, 1: 3 - cls, 9: 3 - cls}[key]
        parity = 0 if key == "s" else (key + 1) % 2
        slots = pl.ds(0, 4) if key == "s" else pl.ds(*u_slots(key, parity))
        return su.at[c, slots], ub.at[row, parity, slots], H_UX + SLOT[key]

    def stand_in(key, kind):
        source, target, number = stand_views(key, kind, layer)
        if key == "s":
            ok = (stand_up & (layer == 1)) | (stand_down & (layer == 0))
        else:
            ok = stand_up if REACH[key][0] else stand_down
        copy = pltpu.make_async_remote_copy(
            src_ref=source, dst_ref=target,
            send_sem=send.at[STAND + STOOD.index((kind, key))], recv_sem=recv.at[number],
            device_id=mate, device_id_type=MESH)
        pl.when(ok)(copy.start)
        started.append((copy, ok))

    def stand_in_y(key):
        goes_up = REACH[key][0]
        row = layer + (2 if key == 2 else 0)
        slots = pl.ds(*u_slots(key, 0))
        copy = pltpu.make_async_remote_copy(
            src_ref=su.at[3 if key == 2 else 2, slots],
            dst_ref=ub.at[row if goes_up else 8 + row, 0, slots],
            send_sem=send.at[STAND + len(STOOD) + SLOT[key]], recv_sem=recv.at[H_UY + SLOT[key]],
            device_id=other_mate, device_id_type=MESH)
        ok = stand_up if goes_up else stand_down
        pl.when(ok)(copy.start)
        started.append((copy, ok))

    def reach_p(key):
        if key == "s":
            push(pb.at[4 + 3 * lam, pl.ds(lam, 7)], pb.at[8 - 5 * lam, pl.ds(lam, 7)],
                 H_P + SLOT[key], special, may_send(key, "x"))
            return
        goes_up, o0, n = REACH[key][:3]
        row = key + 1 - lam if goes_up else key - 7 - lam
        push(pb.at[4 + row, pl.ds(o0, n)], pb.at[row if goes_up else 8 + row, pl.ds(o0, n)],
             H_P + SLOT[key], up if goes_up else down,
             may_send(key, "x" if key in (1, 9) else "y"))

    def got_p(key):
        if key == "s":
            got(pb.at[3 + 5 * lam, pl.ds(1 - lam, 7)], H_P + SLOT[key], comes(key))
            return
        _, o0, n = REACH[key][:3]
        got(pb.at[key + lam, pl.ds(o0, n)], H_P + SLOT[key], comes(key))

    def u_slots(key, parity):
        return REACH[key][3 + 2 * parity], REACH[key][4 + 2 * parity]

    def reach_u(key, cls):
        base = H_UX if cls == "x" else H_UY
        if key == "s":
            parity = 0 if cls == "x" else 1
            push(ub.at[4 + 3 * lam, parity], ub.at[8 - 5 * lam, parity],
                 base + SLOT[key], special, may_send(key, cls))
            return
        goes_up = REACH[key][0]
        parity = (key + 1) % 2 if cls == "x" else key % 2
        m0, n = u_slots(key, parity)
        row = key + 1 - lam if goes_up else key - 7 - lam
        push(ub.at[4 + row, parity, pl.ds(m0, n)],
             ub.at[row if goes_up else 8 + row, parity, pl.ds(m0, n)],
             base + SLOT[key], up if goes_up else down,
             may_send(key, "x" if key in (0, 8, 2) else cls))

    def got_u(key, classes=("x", "y")):
        for cls in classes:
            base = H_UX if cls == "x" else H_UY
            if key == "s":
                got(ub.at[3 + 5 * lam, 0 if cls == "x" else 1], base + SLOT[key], comes(key))
                continue
            parity = (key + 1) % 2 if cls == "x" else key % 2
            m0, n = u_slots(key, parity)
            got(ub.at[key + lam, parity, pl.ds(m0, n)], base + SLOT[key], comes(key))

    special = tuple(jnp.where(lam == 1, a, b) for a, b in zip(up, down))

    def t_step(k, part=None):
        lo, hi = max(0, k - 4), min(9, k + 3)
        width = hi - lo + 1
        rows = []
        if k < 8 and part != 1:
            rows.append(ub[4 + lam, k % 2, k // 2])
        if k >= 2 and part != 0:
            rows.append(ub[6 + lam, k % 2, (k - 2) // 2])
        a = rows[0] if len(rows) == 1 else jnp.concatenate(rows, axis=0)
        r0 = 0 if k < 8 and part != 1 else B
        r1 = 2 * B if k >= 2 and part != 0 else B
        ah, al = split(a)
        both = jnp.concatenate([ah, al], axis=1)
        for w0 in range(0, width, 4):
            w1 = min(width, w0 + 4)
            b = jnp.concatenate(
                [pb[k + lam, lo + w - k + 4] for w in range(w0, w1)], axis=1)
            bh, bl = split(b)
            value = dot(both, jnp.concatenate([bh, bh], axis=0)) + dot(ah, bl)
            t2[r0:r1, (lo + w0) * B:(lo + w1) * B] += value

    def o_step(k, send_out):
        lo, hi = max(0, k - 4), min(9, k + 3)
        r0, r1 = (0 if k < 8 else B), (2 * B if k >= 2 else B)
        b = jnp.concatenate(
            [ub[lam + k, (j - k + 4) % 2, (j - k + 4) // 2] for j in range(lo, hi + 1)], axis=1)
        bh, bl = split(b)
        window = slice(lo * B, (hi + 1) * B)
        ah = th[r0:r1, window]
        value = dot_t(ah, bh) + dot_t(ah, bl) + dot_t(tl[r0:r1, window], bh)
        for a in range(2):
            o = k - 2 * a
            if 0 <= o < NO:
                block = value[a * B - r0:(a + 1) * B - r0]
                ob[a, o] = block * mb[1, pl.ds(a * 8 + o, 1), :]
                send_out(a, o)

    def finish_t(parts):
        for a in parts:
            for j in range(10):
                o = j - 2 * a
                spot = (slice(a * B, (a + 1) * B), slice(j * B, (j + 1) * B))
                if 0 <= o < NO:
                    row = (lam + 2 * a) * 4 + o // 2
                    value = t2[spot] * mb[0 if o % 2 == 0 else 2, pl.ds(row, 1), :]
                    high, low = split(value)
                else:
                    high = low = jnp.zeros((B, B), BF16)
                th[spot] = high
                tl[spot] = low

    def run(swap, early, steps, at_end=True):
        started.clear()
        seen = set()

        def swapped(n):
            kind, c = ORDER[n]
            if swap:
                if kind == "p":
                    got(p_chunk(lam, c), S0_P + c)
                else:
                    got(u_chunk(lam, c), S0_U + c)

        def send_on(n):
            kind, c = ORDER[n]
            swapped(n)
            view = (p_chunk if kind == "p" else u_chunk)(lam, c)
            push(view, view, (S1_P if kind == "p" else S1_U) + c, partner)
            for key in X_AFTER.get((kind, c), ()):
                (reach_p(key) if kind == "p" else reach_u(key, "x"))

        def arrived(n):
            kind, c = ORDER[n]
            got((p_chunk if kind == "p" else u_chunk)(1 - lam, c),
                (S1_P if kind == "p" else S1_U) + c)
            if swap and n == 1:
                pl.when(far_down)(lambda: pl.semaphore_wait(far, 1))
            for key in Y_AFTER.get((kind, c), ()):
                (reach_p(key) if kind == "p" else reach_u(key, "y"))

        def out_copy(a, o):
            view = out.at[a, 0, o]
            number = OUT + a * 8 + o
            if swap:
                return remote(ob.at[a, o], view, number, pair)
            return pltpu.make_async_copy(ob.at[a, o], view, local.at[number])

        def send_out(a, o):
            out_copy(a, o).start()

        def either(step, zero, one, *rest):
            pl.when(lam == 0)(lambda: step(zero, *rest))
            pl.when(lam == 1)(lambda: step(one, *rest))

        def o(key):
            if key == "s":
                got_u(key)
                either(o_step, 3, 7, send_out)
            elif key == "c2":
                either(o_step, 5, 3, send_out)
            elif key == "c3":
                either(o_step, 7, 5, send_out)
            else:
                if key in REACH:
                    got_u(key, ("y",) if key == 2 and "u" in seen else ("x", "y"))
                o_step(key, send_out)

        def t(key, part=None):
            if part != 1 and (key == "s" or key in REACH) and not (key == 1 and "p" in seen):
                got_p(key)
            if key in EITHER:
                either(t_step, *EITHER[key], part)
            else:
                t_step(key, part)

        for n, (kind, c) in enumerate(ORDER):
            (stage_p if kind == "p" else stage_u)(c, swap)
            if n == 0:
                if swap:
                    push(sm, mb.at[pl.ds(0, 2)], S0_M, pair)
                else:
                    mb[0] = sm[0]
                    mb[1] = sm[1]
            if not swap and n < early:
                send_on(n)
        t2[...] = jnp.zeros_like(t2)
        for step in steps:
            what, key = step[0], step[1:]
            key = int(key) if key.isdigit() else key
            if what == "S":
                send_on(key)
            elif what == "A":
                arrived(key)
            elif what == "G":
                if key == "p":
                    got_p(1)
                else:
                    got_u(2, ("x",))
                seen.add(key)
            elif what == "X" and at_end:
                pl.when(stand_down)(lambda: pl.semaphore_wait(far, 2))
                for kind, k in STOOD:
                    stand_in(k, kind)
                for k in (0, 8, 2):
                    stand_in_y(k)
            elif what == "X":
                pass
            elif what == "M":
                if swap:
                    got(mb.at[pl.ds(0, 2)], S0_M)
                push(mb.at[0], mb.at[2], S1_M, partner)
            elif what in "txy":
                t(key, {"t": None, "x": 0, "y": 1}[what])
            elif what in "TVW":
                if what != "W":
                    got(mb.at[2], S1_M)
                finish_t({"T": (0, 1), "V": (0,), "W": (1,)}[what])
            else:
                o(key)

        for a in range(2):
            for p in range(NO):
                out_copy(a, p).wait()
        for copy, ok in started:
            if ok is None:
                copy.wait_send()
            else:
                pl.when(ok)(copy.wait_send)

    def count(ok):
        return ok.astype(jnp.int32)

    pl.semaphore_wait(
        barrier, 1 + swaps + count(upper) + count(lower & ~far_down) + 2 * count(far_end))

    @pl.when(far_up)
    def _():
        for device in (up, mate, other_mate):
            pl.semaphore_signal(far, inc=1, device_id=device, device_id_type=MESH)

    pl.when(swaps == 0)(lambda: run(False, EARLY, NATIVE))
    ends = near_end | far_end
    pl.when((swaps == 1) & ~ends)(lambda: run(True, 0, SWAPPED[:-12] + INNER, False))
    pl.when((swaps == 1) & ends)(lambda: run(True, 0, SWAPPED))


def on_device(cols, u_values, u_mask, p_values, p_mask, t_mask, out_mask):
    smem = pl.BlockSpec(memory_space=pltpu.SMEM)
    hbm = pl.BlockSpec(memory_space=pltpu.HBM)
    return pl.pallas_call(
        functools.partial(kernel, cols),
        out_shape=jax.ShapeDtypeStruct((2, 1, NO, B, B), F32),
        in_specs=[smem] * 4 + [hbm] * 2,
        out_specs=hbm,
        scratch_shapes=[
            pltpu.VMEM((12, 2, 4, B, B), F32),
            pltpu.VMEM((12, NO, B, B), F32),
            pltpu.VMEM((3, 16, B), F32),
            pltpu.VMEM((4, 4, B, B), F32),
            pltpu.VMEM((2, NO, B, B), F32),
            pltpu.VMEM((2, 16, B), F32),
            pltpu.VMEM((2 * B, 10 * B), F32),
            pltpu.VMEM((2 * B, 10 * B), BF16),
            pltpu.VMEM((2 * B, 10 * B), BF16),
            pltpu.VMEM((2, NO, B, B), F32),
            pltpu.SemaphoreType.DMA((COPIES,)),
            pltpu.SemaphoreType.DMA((COPIES,)),
            pltpu.SemaphoreType.DMA((COPIES,)),
            pltpu.SemaphoreType.DMA((8,)),
            pltpu.SemaphoreType.REGULAR,
        ],
        compiler_params=pltpu.CompilerParams(
            collective_id=0, has_side_effects=True, vmem_limit_bytes=62 << 20),
        cost_estimate=pl.CostEstimate(
            flops=2 * 192 * B**3, bytes_accessed=3 << 20, transcendentals=0),
    )(
        u_mask.transpose(0, 2, 1), p_mask, t_mask.transpose(0, 2, 1), out_mask,
        u_values, p_values,
    )


def solution(mesh):
    placed = (
        P(("row", "col"), None, "layer", None, None),
        P(("row", "col"), None, "layer"),
        P(("row", "col"), "layer", None, None, None),
        P(("row", "col"), "layer", None),
        P(("row", "col"), None, "layer"),
        P(("row", "col"), "layer", None),
    )
    return jax.shard_map(
        functools.partial(on_device, mesh.shape["col"]),
        mesh=mesh,
        in_specs=placed,
        out_specs=P(("row", "col"), "layer", None, None, None),
        check_vma=False,
    )
```

```python
import functools

import jax
import jax.numpy as jnp
from jax import lax
from jax.experimental import pallas as pl
from jax.experimental.pallas import tpu as pltpu
from jax.sharding import PartitionSpec as P

B = 128
NO = 8
F32 = jnp.float32
BF16 = jnp.bfloat16
MESH = pl.DeviceIdType.MESH

S0_P, S0_U, S0_M = 0, 4, 8
S1_P, S1_U, S1_M = 9, 13, 17
H_P, H_UX, H_UY = 18, 24, 30
OUT = 36
STAND = 52
COPIES = 65
EARLY = 4
NATIVE = [
    "M", "A0", "A1", "Gp", "S4", "S5", "A2", "A3", "Gu", "S6", "S7", "t4", "t6", "A4", "A5",
    "t1", "t9", "ts", "tp1", "tp3", "t0", "t8", "t2", "T", "A6", "A7", "o4", "o6", "oc2", "oc3",
    "os", "o1", "o9", "o0", "o8", "o2",
]
SWAPPED = [
    "S0", "X", "S1", "S2", "S3", "M", "A0", "A1", "S4", "S5", "A2", "A3", "S6", "S7", "t4",
    "t6", "t0", "t8", "t2", "A4", "t1", "xs", "xp1", "xp3", "V", "A5", "ys", "yp1", "yp3", "t9",
    "W", "o4", "o6", "A6", "oc2", "o0", "o8", "o2", "A7", "oc3", "os", "o9", "o1",
]
INNER = [
    "o4", "o6", "os", "A6", "oc2", "o9", "o1", "o0", "o8", "A7", "oc3", "o2",
]
ORDER = [("p", 0), ("p", 1), ("p", 2), ("p", 3), ("u", 0), ("u", 1), ("u", 2), ("u", 3)]
STOOD = [("p", "s"), ("p", 1), ("p", 9), ("u", 2), ("u", 0), ("u", 8), ("u", "s"), ("u", 1), ("u", 9)]
X_AFTER = {("u", 0): (0, 8), ("u", 1): (2,), ("p", 3): ("s", 1, 9), ("u", 3): ("s", 1, 9)}
Y_AFTER = {("p", 1): (0, 8), ("p", 3): (2,), ("u", 1): ("s", 1, 9), ("u", 2): (0, 8), ("u", 3): (2,)}

REACH = {
    0: (True, 4, 4, 2, 2, 2, 2),
    1: (True, 3, 5, 2, 2, 1, 3),
    2: (True, 2, 6, 1, 3, 1, 3),
    8: (False, 0, 6, 0, 3, 0, 3),
    9: (False, 0, 5, 0, 3, 0, 2),
}
EITHER = {"s": (3, 7), "p1": (5, 3), "p3": (7, 5)}
SLOT = {0: 0, 1: 1, 2: 2, 8: 3, 9: 4, "s": 5}


def split(x):
    high = x.astype(BF16)
    return high, (x - high.astype(F32)).astype(BF16)


def dot(a, b):
    return jnp.dot(a, b, preferred_element_type=F32)


def dot_t(a, b):
    return lax.dot_general(a, b, (((1,), (1,)), ((), ())), preferred_element_type=F32)


def kernel(cols, um, pm, tm, om, u_in, p_in, out, ub, pb, mb, su, sp, sm, t2, th, tl, ob,
           send, recv, local, load, far):
    core = lax.axis_index("row")
    col = lax.axis_index("col")
    layer = lax.axis_index("layer")
    half = col % 2
    quad = col // 2
    quads = cols // 2
    lam = (layer + core + half) % 2
    swaps = (core + half) % 2
    slabs = 4 * quads
    total = 4 * slabs
    first_row = 4 * (core * cols + col)

    def place(index):
        index = (index + slabs) % slabs
        h = index % 2
        q = index // 2
        p = q // quads
        return (h, (q % quads) * 2 + p, (1 - lam + h + p) % 2)

    chain = (half * quads + quad) * 2 + core
    up = place(chain + 1)
    down = place(chain - 1)
    partner = (core, col, 1 - layer)
    pair = (1 - core, quad * 2 + 1 - half, 1 - layer)

    def remote(src, dst, number, device):
        return pltpu.make_async_remote_copy(
            src_ref=src, dst_ref=dst, send_sem=send.at[number], recv_sem=recv.at[number],
            device_id=device, device_id_type=MESH)

    started = []

    def push(src, dst, number, device, ok=None):
        copy = remote(src, dst, number, device)
        started.append((copy, ok))
        if ok is None:
            copy.start()
        else:
            pl.when(ok)(copy.start)

    def got(view, number, ok=None):
        copy = remote(view, view, number, partner)
        if ok is None:
            copy.wait_recv()
        else:
            pl.when(ok)(copy.wait_recv)

    def keep(mask, index, column):
        ok = (column >= 0) & (column < total)
        return jnp.where(ok, mask[index], 0).astype(F32)

    last = quads - 1
    lower = chain != 0
    upper = chain != slabs - 1
    x_up = (core != 1) | (quad != last)
    x_down = (core != 0) | (quad != 0)
    stand_up = (swaps == 1) & (half == 1) & (quad == last)
    stand_down = (swaps == 1) & (half == 0) & (quad == 0)
    mate = (core, (last - quad) * 2 + half, layer)
    other_mate = (core, (last - quad) * 2 + half, 1 - layer)

    def p_chunk(cls, c):
        return pb.at[4 + cls + 2 * (c // 2), pl.ds(4 * (c % 2), 4)]

    def u_chunk(cls, c):
        row = [1 - cls, 3 - cls, cls, cls + 2][c]
        return ub.at[4 + row, [1, 1, 0, 0][c]]

    barrier = pltpu.get_barrier_semaphore()
    near_end = (swaps == 1) & (quad == 0)
    far_end = (swaps == 1) & (quad == last)
    far_down = near_end & (half == 1)
    far_up = far_end & (half == 0)

    def greet(device, ok=None):
        def signal():
            pl.semaphore_signal(barrier, inc=1, device_id=device, device_id_type=MESH)

        if ok is None:
            signal()
        else:
            pl.when(ok)(signal)

    greet(partner)
    greet(up, upper & ~far_up)
    greet(down, lower)
    greet(pair, swaps == 1)
    greet(mate, near_end)
    greet(other_mate, near_end)

    def p_stage(c):
        return sp.at[c // 2, pl.ds(4 * (c % 2), 4)]

    def u_row(c):
        return [1 - layer, 3 - layer, layer, layer + 2][c]

    def loads(c):
        yield pltpu.make_async_copy(
            p_in.at[c // 2, 0, pl.ds(4 * (c % 2), 4)], p_stage(c), load.at[c])
        yield pltpu.make_async_copy(
            u_in.at[u_row(c), pl.ds(0, 4), 0], su.at[c], load.at[4 + c])

    p_loads, u_loads = zip(*[tuple(loads(c)) for c in range(4)])
    for copy in p_loads + u_loads:
        copy.start()

    def stage_p(c, swap):
        a, o0 = c // 2, 4 * (c % 2)
        p_loads[c].wait()

        @pl.loop(0, 4)
        def _(s):
            column = first_row + layer + 2 * a - 4 + o0 + s
            value = sp[a, o0 + s] * keep(pm, (a, 0, o0 + s), column)
            if swap:
                sp[a, o0 + s] = value
            else:
                pb[4 + layer + 2 * a, o0 + s] = value

        if swap:
            push(p_stage(c), p_chunk(layer, c), S0_P + c, pair)

    def stage_u(c, swap):
        row = u_row(c)
        u_loads[c].wait()

        @pl.loop(0, 4)
        def _(s):
            column = first_row + row - 4 + [1, 1, 0, 0][c] + 2 * s
            value = su[c, s] * keep(um, (row, 0, s), column)
            if swap:
                su[c, s] = value
            else:
                ub[4 + row, [1, 1, 0, 0][c], s] = value

        if swap:
            push(su.at[c], u_chunk(layer, c), S0_U + c, pair)

    @pl.loop(0, 16)
    def _(s):
        row, m = s // 4, s % 4
        column = first_row + row - 4 + (layer + row) % 2 + 2 * m
        sm[0, pl.ds(s, 1), :] = jnp.full((1, B), keep(tm, (row, 0, m), column), F32)
        a, o = s // 8, s % 8
        column = first_row + layer + 2 * a - 4 + o
        sm[1, pl.ds(s, 1), :] = jnp.full((1, B), keep(om, (a, 0, o), column), F32)

    def clear(row):
        @pl.loop(row, row + 4)
        def _(r):
            @pl.loop(0, NO)
            def _(o):
                pb[r, o] = jnp.zeros((B, B), F32)
                ub[r, o // 4, o % 4] = jnp.zeros((B, B), F32)

    @pl.when(chain == 0)
    def _():
        clear(0)

    @pl.when(chain == slabs - 1)
    def _():
        clear(8)

    def may_send(key, cls):
        above, below = (x_up, x_down) if cls == "x" else (upper, lower)
        if key == "s":
            return ((lam == 1) & above) | ((lam == 0) & below)
        return above if REACH[key][0] else below

    def comes(key):
        if key == "s":
            return ((lam == 0) & lower) | ((lam == 1) & upper)
        return lower if REACH[key][0] else upper

    def stand_views(key, kind, cls):
        if key == "s":
            source, row = None, 8 - 5 * cls
        else:
            goes_up = REACH[key][0]
            source = key + 1 - cls if goes_up else key - 7 - cls
            row = source if goes_up else 8 + source
        if kind == "p":
            a = cls if key == "s" else 1 - cls
            blocks = pl.ds(cls, 7) if key == "s" else pl.ds(*REACH[key][1:3])
            return sp.at[a, blocks], pb.at[row, blocks], H_P + SLOT[key]
        c = {"s": 2 + cls, 0: 0, 8: 0, 2: 1, 1: 3 - cls, 9: 3 - cls}[key]
        parity = 0 if key == "s" else (key + 1) % 2
        slots = pl.ds(0, 4) if key == "s" else pl.ds(*u_slots(key, parity))
        return su.at[c, slots], ub.at[row, parity, slots], H_UX + SLOT[key]

    def stand_in(key, kind):
        source, target, number = stand_views(key, kind, layer)
        if key == "s":
            ok = (stand_up & (layer == 1)) | (stand_down & (layer == 0))
        else:
            ok = stand_up if REACH[key][0] else stand_down
        copy = pltpu.make_async_remote_copy(
            src_ref=source, dst_ref=target,
            send_sem=send.at[STAND + STOOD.index((kind, key))], recv_sem=recv.at[number],
            device_id=mate, device_id_type=MESH)
        pl.when(ok)(copy.start)
        started.append((copy, ok))

    def stand_in_y(key):
        goes_up = REACH[key][0]
        row = layer + (2 if key == 2 else 0)
        slots = pl.ds(*u_slots(key, 0))
        copy = pltpu.make_async_remote_copy(
            src_ref=su.at[3 if key == 2 else 2, slots],
            dst_ref=ub.at[row if goes_up else 8 + row, 0, slots],
            send_sem=send.at[STAND + len(STOOD) + SLOT[key]], recv_sem=recv.at[H_UY + SLOT[key]],
            device_id=other_mate, device_id_type=MESH)
        ok = stand_up if goes_up else stand_down
        pl.when(ok)(copy.start)
        started.append((copy, ok))

    def reach_p(key):
        if key == "s":
            push(pb.at[4 + 3 * lam, pl.ds(lam, 7)], pb.at[8 - 5 * lam, pl.ds(lam, 7)],
                 H_P + SLOT[key], special, may_send(key, "x"))
            return
        goes_up, o0, n = REACH[key][:3]
        row = key + 1 - lam if goes_up else key - 7 - lam
        push(pb.at[4 + row, pl.ds(o0, n)], pb.at[row if goes_up else 8 + row, pl.ds(o0, n)],
             H_P + SLOT[key], up if goes_up else down,
             may_send(key, "x" if key in (1, 9) else "y"))

    def got_p(key):
        if key == "s":
            got(pb.at[3 + 5 * lam, pl.ds(1 - lam, 7)], H_P + SLOT[key], comes(key))
            return
        _, o0, n = REACH[key][:3]
        got(pb.at[key + lam, pl.ds(o0, n)], H_P + SLOT[key], comes(key))

    def u_slots(key, parity):
        return REACH[key][3 + 2 * parity], REACH[key][4 + 2 * parity]

    def reach_u(key, cls):
        base = H_UX if cls == "x" else H_UY
        if key == "s":
            parity = 0 if cls == "x" else 1
            push(ub.at[4 + 3 * lam, parity], ub.at[8 - 5 * lam, parity],
                 base + SLOT[key], special, may_send(key, cls))
            return
        goes_up = REACH[key][0]
        parity = (key + 1) % 2 if cls == "x" else key % 2
        m0, n = u_slots(key, parity)
        row = key + 1 - lam if goes_up else key - 7 - lam
        push(ub.at[4 + row, parity, pl.ds(m0, n)],
             ub.at[row if goes_up else 8 + row, parity, pl.ds(m0, n)],
             base + SLOT[key], up if goes_up else down,
             may_send(key, "x" if key in (0, 8, 2) else cls))

    def got_u(key, classes=("x", "y")):
        for cls in classes:
            base = H_UX if cls == "x" else H_UY
            if key == "s":
                got(ub.at[3 + 5 * lam, 0 if cls == "x" else 1], base + SLOT[key], comes(key))
                continue
            parity = (key + 1) % 2 if cls == "x" else key % 2
            m0, n = u_slots(key, parity)
            got(ub.at[key + lam, parity, pl.ds(m0, n)], base + SLOT[key], comes(key))

    special = tuple(jnp.where(lam == 1, a, b) for a, b in zip(up, down))

    def t_step(k, part=None):
        lo, hi = max(0, k - 4), min(9, k + 3)
        width = hi - lo + 1
        rows = []
        if k < 8 and part != 1:
            rows.append(ub[4 + lam, k % 2, k // 2])
        if k >= 2 and part != 0:
            rows.append(ub[6 + lam, k % 2, (k - 2) // 2])
        a = rows[0] if len(rows) == 1 else jnp.concatenate(rows, axis=0)
        r0 = 0 if k < 8 and part != 1 else B
        r1 = 2 * B if k >= 2 and part != 0 else B
        ah, al = split(a)
        both = jnp.concatenate([ah, al], axis=1)
        for w0 in range(0, width, 4):
            w1 = min(width, w0 + 4)
            b = jnp.concatenate(
                [pb[k + lam, lo + w - k + 4] for w in range(w0, w1)], axis=1)
            bh, bl = split(b)
            value = dot(both, jnp.concatenate([bh, bh], axis=0)) + dot(ah, bl)
            t2[r0:r1, (lo + w0) * B:(lo + w1) * B] += value

    def o_step(k, send_out):
        lo, hi = max(0, k - 4), min(9, k + 3)
        r0, r1 = (0 if k < 8 else B), (2 * B if k >= 2 else B)
        b = jnp.concatenate(
            [ub[lam + k, (j - k + 4) % 2, (j - k + 4) // 2] for j in range(lo, hi + 1)], axis=1)
        bh, bl = split(b)
        window = slice(lo * B, (hi + 1) * B)
        ah = th[r0:r1, window]
        value = dot_t(ah, bh) + dot_t(ah, bl) + dot_t(tl[r0:r1, window], bh)
        for a in range(2):
            o = k - 2 * a
            if 0 <= o < NO:
                block = value[a * B - r0:(a + 1) * B - r0]
                ob[a, o] = block * mb[1, pl.ds(a * 8 + o, 1), :]
                send_out(a, o)

    def finish_t(parts):
        for a in parts:
            for j in range(10):
                o = j - 2 * a
                spot = (slice(a * B, (a + 1) * B), slice(j * B, (j + 1) * B))
                if 0 <= o < NO:
                    row = (lam + 2 * a) * 4 + o // 2
                    value = t2[spot] * mb[0 if o % 2 == 0 else 2, pl.ds(row, 1), :]
                    high, low = split(value)
                else:
                    high = low = jnp.zeros((B, B), BF16)
                th[spot] = high
                tl[spot] = low

    def run(swap, early, steps, at_end=True):
        started.clear()
        seen = set()

        def swapped(n):
            kind, c = ORDER[n]
            if swap:
                if kind == "p":
                    got(p_chunk(lam, c), S0_P + c)
                else:
                    got(u_chunk(lam, c), S0_U + c)

        def send_on(n):
            kind, c = ORDER[n]
            swapped(n)
            view = (p_chunk if kind == "p" else u_chunk)(lam, c)
            push(view, view, (S1_P if kind == "p" else S1_U) + c, partner)
            for key in X_AFTER.get((kind, c), ()):
                (reach_p(key) if kind == "p" else reach_u(key, "x"))

        def arrived(n):
            kind, c = ORDER[n]
            got((p_chunk if kind == "p" else u_chunk)(1 - lam, c),
                (S1_P if kind == "p" else S1_U) + c)
            if swap and n == 1:
                pl.when(far_down)(lambda: pl.semaphore_wait(far, 1))
            for key in Y_AFTER.get((kind, c), ()):
                (reach_p(key) if kind == "p" else reach_u(key, "y"))

        def out_copy(a, o):
            view = out.at[a, 0, o]
            number = OUT + a * 8 + o
            if swap:
                return remote(ob.at[a, o], view, number, pair)
            return pltpu.make_async_copy(ob.at[a, o], view, local.at[number])

        def send_out(a, o):
            out_copy(a, o).start()

        def either(step, zero, one, *rest):
            pl.when(lam == 0)(lambda: step(zero, *rest))
            pl.when(lam == 1)(lambda: step(one, *rest))

        def o(key):
            if key == "s":
                got_u(key)
                either(o_step, 3, 7, send_out)
            elif key == "c2":
                either(o_step, 5, 3, send_out)
            elif key == "c3":
                either(o_step, 7, 5, send_out)
            else:
                if key in REACH:
                    got_u(key, ("y",) if key == 2 and "u" in seen else ("x", "y"))
                o_step(key, send_out)

        def t(key, part=None):
            if part != 1 and (key == "s" or key in REACH) and not (key == 1 and "p" in seen):
                got_p(key)
            if key in EITHER:
                either(t_step, *EITHER[key], part)
            else:
                t_step(key, part)

        for n, (kind, c) in enumerate(ORDER):
            if swap:
                (stage_p if kind == "p" else stage_u)(c, swap)
            if n == 0:
                if swap:
                    push(sm, mb.at[pl.ds(0, 2)], S0_M, pair)
                else:
                    mb[0] = sm[0]
                    mb[1] = sm[1]
            if not swap and n < early:
                send_on(n)
        t2[...] = jnp.zeros_like(t2)
        for step in steps:
            what, key = step[0], step[1:]
            key = int(key) if key.isdigit() else key
            if what == "S":
                send_on(key)
            elif what == "A":
                arrived(key)
            elif what == "G":
                if key == "p":
                    got_p(1)
                else:
                    got_u(2, ("x",))
                seen.add(key)
            elif what == "X" and at_end:
                pl.when(stand_down)(lambda: pl.semaphore_wait(far, 2))
                for kind, k in STOOD:
                    stand_in(k, kind)
                for k in (0, 8, 2):
                    stand_in_y(k)
            elif what == "X":
                pass
            elif what == "M":
                if swap:
                    got(mb.at[pl.ds(0, 2)], S0_M)
                push(mb.at[0], mb.at[2], S1_M, partner)
            elif what in "txy":
                t(key, {"t": None, "x": 0, "y": 1}[what])
            elif what in "TVW":
                if what != "W":
                    got(mb.at[2], S1_M)
                finish_t({"T": (0, 1), "V": (0,), "W": (1,)}[what])
            else:
                o(key)

        for a in range(2):
            for p in range(NO):
                out_copy(a, p).wait()
        for copy, ok in started:
            if ok is None:
                copy.wait_send()
            else:
                pl.when(ok)(copy.wait_send)

    def count(ok):
        return ok.astype(jnp.int32)

    @pl.when(swaps == 0)
    def _():
        for kind, c in ORDER:
            (stage_p if kind == "p" else stage_u)(c, False)

    pl.semaphore_wait(
        barrier, 1 + swaps + count(upper) + count(lower & ~far_down) + 2 * count(far_end))

    @pl.when(far_up)
    def _():
        for device in (up, mate, other_mate):
            pl.semaphore_signal(far, inc=1, device_id=device, device_id_type=MESH)

    pl.when(swaps == 0)(lambda: run(False, EARLY, NATIVE))
    ends = near_end | far_end
    pl.when((swaps == 1) & ~ends)(lambda: run(True, 0, SWAPPED[:-12] + INNER, False))
    pl.when((swaps == 1) & ends)(lambda: run(True, 0, SWAPPED))


def on_device(cols, u_values, u_mask, p_values, p_mask, t_mask, out_mask):
    smem = pl.BlockSpec(memory_space=pltpu.SMEM)
    hbm = pl.BlockSpec(memory_space=pltpu.HBM)
    return pl.pallas_call(
        functools.partial(kernel, cols),
        out_shape=jax.ShapeDtypeStruct((2, 1, NO, B, B), F32),
        in_specs=[smem] * 4 + [hbm] * 2,
        out_specs=hbm,
        scratch_shapes=[
            pltpu.VMEM((12, 2, 4, B, B), F32),
            pltpu.VMEM((12, NO, B, B), F32),
            pltpu.VMEM((3, 16, B), F32),
            pltpu.VMEM((4, 4, B, B), F32),
            pltpu.VMEM((2, NO, B, B), F32),
            pltpu.VMEM((2, 16, B), F32),
            pltpu.VMEM((2 * B, 10 * B), F32),
            pltpu.VMEM((2 * B, 10 * B), BF16),
            pltpu.VMEM((2 * B, 10 * B), BF16),
            pltpu.VMEM((2, NO, B, B), F32),
            pltpu.SemaphoreType.DMA((COPIES,)),
            pltpu.SemaphoreType.DMA((COPIES,)),
            pltpu.SemaphoreType.DMA((COPIES,)),
            pltpu.SemaphoreType.DMA((8,)),
            pltpu.SemaphoreType.REGULAR,
        ],
        compiler_params=pltpu.CompilerParams(
            collective_id=0, has_side_effects=True, vmem_limit_bytes=62 << 20),
        cost_estimate=pl.CostEstimate(
            flops=2 * 192 * B**3, bytes_accessed=3 << 20, transcendentals=0),
    )(
        u_mask.transpose(0, 2, 1), p_mask, t_mask.transpose(0, 2, 1), out_mask,
        u_values, p_values,
    )


def solution(mesh):
    placed = (
        P(("row", "col"), None, "layer", None, None),
        P(("row", "col"), None, "layer"),
        P(("row", "col"), "layer", None, None, None),
        P(("row", "col"), "layer", None),
        P(("row", "col"), None, "layer"),
        P(("row", "col"), "layer", None),
    )
    return jax.shard_map(
        functools.partial(on_device, mesh.shape["col"]),
        mesh=mesh,
        in_specs=placed,
        out_specs=P(("row", "col"), "layer", None, None, None),
        check_vma=False,
    )
```
